512 devices in a mesh: gx: 16 (over z, core), yz: 8 (over y), body: 4 (over x).
Axes of the slice: x: 4, y: 8, z: 8, core: 2. Of those that a mesh axis runs over, the one named last changes fastest.
Arguments:
- fluid_pos: float32 [3, 32, 16, 8, 128], P(None, 'gx', 'yz', 'body'), may hold values from 0 to 1
- fluid_count: int32 [32, 16, 8], P('gx', 'yz', 'body'), may hold values from 64 to 128
- body_shape: float32 [3, 12288, 128], P(None, ('gx', 'yz', 'body')), may hold values from -2.5 to 2.5
- body_anchor: float32 [3, 12288, 8], P(None, ('gx', 'yz', 'body')), may hold values from -0.5 to 1.5
- body_dest: int32 [12288, 1], P(('gx', 'yz', 'body')), may hold values from 0 to 15; in each aligned block of 24 rows (0 to 23, 24 to 47, ...) at most 3 rows name the same one
- body_cell: int32 [12288, 8], P(('gx', 'yz', 'body')), may hold values from 0 to 7, as said below
Outputs:
- fluid_density: float32 [32, 16, 8, 128], P('gx', 'yz', 'body')
- fluid_accel: float32 [3, 32, 16, 8, 128], P(None, 'gx', 'yz', 'body')
- body_load: float32 [6, 12288], P(None, ('gx', 'yz', 'body'))
The draws below stay inside these ranges and needn't reach their ends.
Inputs may be any that keep to these rules, and one draw needn't show every extreme that they name: `fluid_count`: slots at or past a cell's count are padding. `body_dest`: the rows of one device name any index at most 3 times, a bound that some block reaches. `body_cell`: a row lists the local cells ((a0 + a) % 2, (e0 + e) % 2, (f0 + f) % 2), entry k having a = k // 4, e = (k // 2) % 2, f = k % 2.
All inputs are finite; a program needn't handle non-finite values.
Results may differ from the reference program's by a relative error of at most 0.0003.
Values sent between devices are 32-bit elements; how exact they have to be, the bound alone decides.
No kernel may reach another device: no remote copies, remote signals or barrier semaphores. Data moves between devices by JAX's collectives and lax.ppermute only.
A program may use at most 64 MiB of HBM per device.

```python
import math
import jax
import jax.numpy as jnp
import numpy as np
from jax import lax

CELLS_X = 2
CELLS_Y = 2
CELLS_Z = 2
SLOTS = 128
BODY_PARTS = 128
COVER = 8
CAPACITY = 3
BODIES_DEV = 24
BODIES = 12288
GRID_X = 32
GRID_Y = 16
GRID_Z = 8
N_GX = 16
N_YZ = 8
N_BODY = 4


def draw_body_anchor(key, part):
    centre = jax.random.uniform(key, (3, BODIES, 1), jnp.float32, 0.5, 1.5)
    steps = jnp.arange(COVER, dtype=jnp.int32)
    offsets = jnp.stack([steps // 4, steps // 2 % 2, steps % 2]).astype(jnp.float32)
    return centre - offsets[:, None, :]


def draw_body_cell(key, part):
    key_x, key_y, key_z = jax.random.split(jax.random.fold_in(key, 7), 3)
    corner_x = jax.random.randint(key_x, (BODIES, 1), 0, CELLS_X)
    corner_y = jax.random.randint(key_y, (BODIES, 1), 0, CELLS_Y)
    corner_z = jax.random.randint(key_z, (BODIES, 1), 0, CELLS_Z)
    steps = jnp.arange(COVER, dtype=jnp.int32)[None, :]
    place_x = (corner_x + steps // 4) % CELLS_X
    place_y = (corner_y + steps // 2 % 2) % CELLS_Y
    place_z = (corner_z + steps % 2) % CELLS_Z
    return ((place_x * CELLS_Y + place_y) * CELLS_Z + place_z).astype(jnp.int32)


def set_ends(drawn, rng, low, high):
    longest = drawn.shape.index(max(drawn.shape))
    spots = []
    for shift in (0, 1):
        where = [jax.random.randint(jax.random.fold_in(rng, axis), (), 0, length) for axis, length in enumerate(drawn.shape)]
        where[longest] = (where[longest] + shift) % drawn.shape[longest]
        spots.append(tuple(where))
    return drawn.at[spots[0]].set(low).at[spots[1]].set(high)


def levels(stream_key, shape, cuts, smallest, top_value):
    loudness = 1.0
    for axis_at, blocks in cuts:
        steps = jax.random.uniform(jax.random.fold_in(jax.random.fold_in(stream_key, 6), axis_at), (blocks,), jnp.float32, smallest / len(cuts), top_value / len(cuts))
        loudness = loudness * jnp.repeat(jnp.exp(steps), shape[axis_at] // blocks).reshape((-1,) + (1,) * (len(shape) - 1 - axis_at))
    return loudness


def assign_block(own_key, own, number, rows, amount, top, bound, lean):
    order = jax.random.permutation(own_key, amount)
    crowded, common = portions_of(amount, rows * top, bound, lean, True), portions_of(amount, rows * top, bound, lean, False)
    places = jnp.arange(amount)

    def named(tallies, offset_by):
        used = int((tallies > 0).sum())
        fixed = max(1, used // 4)
        moved = fixed + (places - fixed + offset_by * (used - fixed)) % max(1, amount - fixed)
        return jnp.zeros((amount,), jnp.int32).at[order[jnp.where(places < fixed, places, moved)]].set(jnp.asarray(tallies, jnp.int32))

    tallies = jnp.where(number % 4 == 0, named(crowded, number // 4), named(common, number - number // 4 - 1))
    mixed = jax.random.permutation(jax.random.fold_in(own, 3), amount)
    source_of, sink = mixed[0:amount // 2 * 2:2], mixed[1:amount // 2 * 2:2]
    room = jnp.minimum(tallies[source_of] - 1, bound - tallies[sink]) // 2
    room = jnp.where((source_of == order[0]) | (sink == order[0]) | (tallies[sink] == 0), 0, jnp.maximum(room, 0))
    moved = jax.random.randint(jax.random.fold_in(own, 4), (amount // 2,), 0, 1 << 20) % (room + 1)
    tallies = tallies.at[source_of].add(-moved).at[sink].add(moved)
    members = jnp.searchsorted(jnp.cumsum(tallies), jnp.arange(rows * top), side="right").astype(jnp.int32)
    grid = members.reshape(top, rows).T
    grid = grid[jax.random.permutation(jax.random.fold_in(own, 1), rows)]
    offset_by = jax.random.randint(jax.random.fold_in(own, 2), (rows, 1), 0, top)
    return jnp.take_along_axis(grid, (jnp.arange(top)[None, :] + offset_by) % top, axis=1)


def portions_of(amount, total, bound, skew, full):
    portions = [(1 << 20) // math.isqrt(standing ** skew) + 1 for standing in range(1, amount + 1)]
    largest = bound if full else min(bound, max(-(-total // amount), total * portions[0] // sum(portions)))
    least = 1 if total - largest >= amount - 1 else 0
    given, surplus = [largest] + [least] * (amount - 1), total - largest - least * (amount - 1)
    while surplus > 0:
        candidates = [i for i in range(1, amount) if given[i] < largest] or [i for i in range(1, amount) if given[i] < bound]
        mass, remaining = sum([portions[i] for i in candidates]), surplus
        for i in candidates:
            addition = min(bound - given[i], max(1, remaining * portions[i] // mass), surplus)
            given[i] = given[i] + addition
            surplus = surplus - addition
    return np.array(given)


def bell_draw(rng, dims, deviation, reach, shards=(), kind=jnp.bfloat16):
    array = deviation * jax.random.normal(rng, dims, jnp.float32)
    if shards:
        array = array * levels(rng, dims, shards, -0.22, 0.18)
    return jnp.clip(array, -reach, reach).astype(kind)


def setup_inputs(seed: int = 0) -> dict:
    key_of = jax.random.split(jax.random.key(seed), 7)
    fluid_pos = jnp.clip(1.0 * jax.random.uniform(key_of[0], (3, GRID_X, GRID_Y, GRID_Z, SLOTS), jnp.float32) ** levels(key_of[0], (3, GRID_X, GRID_Y, GRID_Z, SLOTS), ((1, 16), (2, 8), (3, 4)), -0.2, 0.2), 0.0, 1.0)
    fluid_count = set_ends(jax.random.randint(key_of[1], (GRID_X, GRID_Y, GRID_Z), SLOTS // 2, SLOTS + 1), jax.random.fold_in(key_of[1], 1), SLOTS // 2, SLOTS).astype(jnp.int32)
    body_shape = bell_draw(key_of[2], (3, BODIES, BODY_PARTS), 0.4, 2.5, ((1, 512),), jnp.float32)
    body_anchor = draw_body_anchor(jax.random.fold_in(key_of[6], 71), 0)
    body_dest_keys = jax.random.split(jax.random.fold_in(key_of[4], 1), BODIES // BODIES_DEV)
    body_dest_turns = jax.random.permutation(jax.random.fold_in(key_of[4], 3), BODIES // BODIES_DEV)
    body_dest = jax.vmap(lambda own, number: assign_block(jax.random.fold_in(key_of[4], 2), own, number, BODIES_DEV, N_GX, 1, CAPACITY, 2))(body_dest_keys, body_dest_turns).reshape((BODIES, 1))
    body_cell = draw_body_cell(jax.random.fold_in(key_of[6], 71), 0)
    return {"fluid_pos": fluid_pos, "fluid_count": fluid_count, "body_shape": body_shape, "body_anchor": body_anchor, "body_dest": body_dest, "body_cell": body_cell}


stencil_steps = [(a, b, c) for a in (-1, 0, 1) for b in (-1, 0, 1) for c in (-1, 0, 1)]


def pair_terms(own_tile, near_tile, stencil):
    gap_parts = [own_tile[m][..., :, None] - near_tile[m][..., None, :] - float(stencil[m]) for m in range(3)]
    spread = jnp.maximum(1.0 - (gap_parts[0] * gap_parts[0] + gap_parts[1] * gap_parts[1] + gap_parts[2] * gap_parts[2]), 0.0)
    return gap_parts, spread


def pressure_of(density, live_mask):
    safe_den = jnp.where(live_mask > 0, density, 1.0)
    return jnp.where(live_mask > 0, (density - 1.0) / (safe_den * safe_den), 0.0)


def cross_arms(arm_vecs, forces):
    return jnp.stack([arm_vecs[:, 1] * forces[:, 2] - arm_vecs[:, 2] * forces[:, 1],
                      arm_vecs[:, 2] * forces[:, 0] - arm_vecs[:, 0] * forces[:, 2],
                      arm_vecs[:, 0] * forces[:, 1] - arm_vecs[:, 1] * forces[:, 0]], axis=1)


def interact(positions, fluid_tiles):
    deltas = positions[:, :, :, None] - fluid_tiles[:, :3, None, :]
    spread = jnp.maximum(1.0 - jnp.sum(deltas * deltas, axis=1), 0.0)
    weight = (24.0 / SLOTS) * (fluid_tiles[:, 3] * fluid_tiles[:, 4])[:, None, :] * spread * spread
    pushed = weight[:, None] * deltas
    return jnp.sum(pushed, axis=3), -jnp.sum(pushed, axis=2)


def reference(fluid_pos, fluid_count, body_shape, body_anchor, body_dest, body_cell):
    live_mask = (jnp.arange(SLOTS, dtype=jnp.int32)[None, None, None, :] < fluid_count[..., None]).astype(jnp.float32)
    packed = jnp.concatenate([fluid_pos, live_mask[None]], axis=0)
    padded = jnp.pad(packed, ((0, 0), (1, 1), (1, 1), (1, 1), (0, 0)))
    columns = jnp.arange(GRID_X, dtype=jnp.int32)

    def density_slab(column):
        own_tile = lax.dynamic_slice_in_dim(padded, column + 1, 1, 1)[:, :, 1:-1, 1:-1]
        summed = jnp.zeros((1, GRID_Y, GRID_Z, SLOTS), jnp.float32)
        for stencil in stencil_steps:
            near_tile = lax.dynamic_slice_in_dim(padded, column + 1 + stencil[0], 1, 1)[:, :, 1 + stencil[1]:1 + stencil[1] + GRID_Y, 1 + stencil[2]:1 + stencil[2] + GRID_Z]
            gap_parts, spread = pair_terms(own_tile, near_tile, stencil)
            summed = summed + jnp.sum(near_tile[3][..., None, :] * spread * spread * spread, axis=-1)
        return summed[0]

    density = live_mask * lax.map(density_slab, columns) / (SLOTS / 2.0)
    pressure = pressure_of(density, live_mask)
    full_tiles = jnp.concatenate([packed, pressure[None]], axis=0)
    padded_full = jnp.pad(full_tiles, ((0, 0), (1, 1), (1, 1), (1, 1), (0, 0)))

    def accel_slab(column):
        own_tile = lax.dynamic_slice_in_dim(padded_full, column + 1, 1, 1)[:, :, 1:-1, 1:-1]
        summed = jnp.zeros((3, 1, GRID_Y, GRID_Z, SLOTS), jnp.float32)
        for stencil in stencil_steps:
            near_tile = lax.dynamic_slice_in_dim(padded_full, column + 1 + stencil[0], 1, 1)[:, :, 1 + stencil[1]:1 + stencil[1] + GRID_Y, 1 + stencil[2]:1 + stencil[2] + GRID_Z]
            gap_parts, spread = pair_terms(own_tile, near_tile, stencil)
            weight = own_tile[3][..., :, None] * near_tile[3][..., None, :] * (own_tile[4][..., :, None] + near_tile[4][..., None, :]) * spread * spread
            summed = summed + jnp.stack([jnp.sum(weight * g, axis=-1) for g in gap_parts])
        return summed[:, 0]

    accel_grid = (12.0 / SLOTS) * jnp.transpose(lax.map(accel_slab, columns), (1, 0, 2, 3, 4))

    cell_total = GRID_X * GRID_Y * GRID_Z
    tile_table = jnp.transpose(full_tiles.reshape(5, cell_total, SLOTS), (1, 0, 2))
    entries = BODIES * COVER
    owner_rows = jnp.arange(entries, dtype=jnp.int32) // COVER
    group_index = jnp.repeat(body_dest[:, 0], COVER)
    owner_device = owner_rows // BODIES_DEV
    owner_yz = (owner_device // N_BODY) % N_YZ
    owner_body = owner_device % N_BODY
    flat_cell = body_cell.reshape(entries)
    cell_x = group_index * CELLS_X + flat_cell // (CELLS_Y * CELLS_Z)
    cell_y = owner_yz * CELLS_Y + (flat_cell // CELLS_Z) % CELLS_Y
    cell_z = owner_body * CELLS_Z + flat_cell % CELLS_Z
    target = ((cell_x * GRID_Y + cell_y) * GRID_Z + cell_z).astype(jnp.int32)
    anchors = jnp.transpose(body_anchor, (1, 2, 0)).reshape(entries, 3)
    shapes = jnp.transpose(body_shape, (1, 0, 2))

    def entry_block(reaction_grid, pieces):
        block_target, block_owner, block_anchor = pieces
        offsets = jnp.take(shapes, block_owner, axis=0)
        fluid_tiles = jnp.take(tile_table, block_target, axis=0)
        forces, reaction = interact(block_anchor[:, :, None] + offsets, fluid_tiles)
        entry_loads = jnp.concatenate([jnp.sum(forces, axis=2), jnp.sum(cross_arms(offsets, forces), axis=2)], axis=1)
        return reaction_grid.at[block_target].add(reaction), entry_loads

    start = jnp.zeros((cell_total, 3, SLOTS), jnp.float32)
    reaction_grid, entry_loads = lax.scan(entry_block, start, (target.reshape(-1, 256), owner_rows.reshape(-1, 256), anchors.reshape(-1, 256, 3)))
    fluid_accel = accel_grid + jnp.transpose(reaction_grid, (1, 0, 2)).reshape(3, GRID_X, GRID_Y, GRID_Z, SLOTS)
    body_load = jnp.transpose(jnp.sum(entry_loads.reshape(BODIES, COVER, 6), axis=1) / BODY_PARTS)
    return density, fluid_accel, body_load
```

```python
import jax
import jax.numpy as jnp
from jax import lax
from jax.experimental import pallas as pl
from jax.experimental.pallas import tpu as pltpu
from jax.sharding import PartitionSpec as P

SLOTS = 128
BODY_PARTS = 128
CAPACITY = 3
FAR = 64.0
ROWS = 32
F32 = jnp.float32
BF16 = jnp.bfloat16


def split3(v):
    high = v.astype(BF16).astype(F32)
    rest = v - high
    mid = rest.astype(BF16).astype(F32)
    return high, mid, rest - mid


def near_rows(coords):
    rows = []
    norm = 0.0
    for v in coords:
        h, m, l = split3(v)
        rows += [h, m, h, l, h, m]
        norm = norm + v * v
    one = jnp.ones_like(norm)
    return rows + list(split3(-norm)) + [one, one, one]


def own_rows(coords):
    rows = []
    norm = 0.0
    for v in coords:
        h, m, l = split3(2.0 * v)
        rows += [h, h, m, h, l, m]
        norm = norm + v * v
    one = jnp.ones_like(norm)
    return rows + [one, one, one] + list(split3(1.0 - norm))


def pack_kernel(pos_ref, count_ref, shape_ref, anchor_ref, dest_ref, cell_ref, out_ref, send_ref, slot_ref, extra_ref, tally_ref):
    bodies = shape_ref.shape[1]
    groups = tally_ref.shape[0]
    lane = lax.broadcasted_iota(jnp.int32, (2, SLOTS), 1)
    row = lax.broadcasted_iota(jnp.int32, (2, SLOTS), 0)
    for a in range(2):
        for e in range(2):
            count = jnp.where(row == 0, count_ref[a, e, 0], count_ref[a, e, 1])
            live = lane < count
            base = 4 * a + 2 * e
            out_ref[0, base:base + 2, :] = jnp.where(live, pos_ref[0, a, e], FAR)
            out_ref[1, base:base + 2, :] = pos_ref[1, a, e]
            out_ref[2, base:base + 2, :] = pos_ref[2, a, e]
    send_ref[...] = jnp.zeros_like(send_ref)
    extra_ref[...] = jnp.concatenate(
        [
            anchor_ref[0],
            anchor_ref[1],
            anchor_ref[2],
            cell_ref[...].astype(F32),
            jnp.ones((bodies, 8), F32),
            jnp.zeros((bodies, SLOTS - 40), F32),
        ],
        axis=1,
    )
    for g in range(groups):
        tally_ref[g] = 0
    for b in range(bodies):
        dest = dest_ref[b, 0]
        rank = tally_ref[dest]
        tally_ref[dest] = rank + 1
        slot = dest * CAPACITY + rank
        slot_ref[b] = slot
        send_ref[slot, 0:3, :] = shape_ref[:, b, :]
        send_ref[slot, 3:4, :] = extra_ref[b:b + 1, :]


def density_kernel(left_ref, mid_ref, right_ref, rho_ref, press_ref, near_ref, coord_ref, own_ref, fb_ref, fa_ref, fr_ref, live_ref, col_ref):
    index = [lax.axis_index(n) for n in ("gx", "yz", "body")]
    size = [lax.axis_size(n) for n in ("gx", "yz", "body")]
    sub = lax.broadcasted_iota(jnp.int32, (8, SLOTS), 0)
    part = [sub // 4, sub // 2 % 2, sub % 2]
    fb_ref[...] = jnp.zeros_like(fb_ref)
    fa_ref[...] = jnp.zeros_like(fa_ref)
    fr_ref[...] = jnp.zeros_like(fr_ref)

    def block(t, carry):
        by = t // 3
        bz = t % 3
        ny = index[1] + by - 1
        nz = index[2] + bz - 1
        inside = (ny >= 0) & (ny < size[1]) & (nz >= 0) & (nz < size[2])
        off_y = (part[1] + 2 * by - 3).astype(F32)
        off_z = (part[2] + 2 * bz - 3).astype(F32)
        for kind in range(2):
            if kind == 0:
                raw = [mid_ref[t, m] for m in range(3)]
                wx = part[0] + 1
                ok = jnp.full((8, SLOTS), inside)
            else:
                raw = [jnp.where(sub >= 4, left_ref[t, m], right_ref[t, m]) for m in range(3)]
                wx = 3 - 3 * part[0]
                ok = jnp.where(sub >= 4, index[0], size[0] - 1 - index[0]) > 0
                ok = ok & inside
            coords = [
                jnp.where(ok, raw[0], FAR) + (wx - 2).astype(F32),
                raw[1] + off_y,
                raw[2] + off_z,
            ]
            for r, v in enumerate(near_rows(coords)):
                fb_ref[8 * r:8 * r + 8, :] = v
            for m in range(3):
                fr_ref[8 * m:8 * m + 8, :] = coords[m]
            if kind == 0:
                for r, v in enumerate(own_rows(coords)):
                    fa_ref[t, 8 * r:8 * r + 8, :] = v
            for c in range(8):
                a, e, f = c // 4, c // 2 % 2, c % 2
                at_x = 1 + a if kind == 0 else 3 - 3 * a
                w = (at_x * 6 + 2 * by + e) * 6 + 2 * bz + f
                near_ref[w] = fb_ref[pl.ds(c, ROWS, stride=8), :].astype(BF16)
                coord_ref[w] = fr_ref[pl.ds(c, 8, stride=8), :]
        return carry

    lax.fori_loop(0, 9, block, 0)

    def turn(r, carry):
        wy = r // 4 % 4 + 1
        wz = r % 4 + 1
        t = wy // 2 * 3 + wz // 2
        c = r // 16 * 4 + wy % 2 * 2 + wz % 2
        own_ref[r] = fa_ref[t, pl.ds(c, ROWS, stride=8), :].T.astype(BF16)
        w = ((r // 16 + 1) * 6 + wy) * 6 + wz
        live_ref[pl.ds(r, 1), :] = coord_ref[w, 0:1, :]
        return carry

    lax.fori_loop(0, 32, turn, 0, unroll=4)
    col_ref[...] = jnp.zeros_like(col_ref)
    lane = lax.broadcasted_iota(jnp.int32, (SLOTS, SLOTS), 1)

    def cell(r, carry):
        w = ((r // 16 + 1) * 6 + r // 4 % 4 + 1) * 6 + r % 4 + 1
        lhs = own_ref[r]
        acc = jnp.zeros((SLOTS, SLOTS), F32)
        steps = [(dx * 6 + dy) * 6 + dz for dx in (-1, 0, 1) for dy in (-1, 0, 1) for dz in (-1, 0, 1)]
        for g in range(0, 27, 2):
            pair = steps[g:g + 2]
            rhs = [near_ref[w + s] for s in pair]
            rhs = jnp.concatenate(rhs, axis=1) if len(rhs) == 2 else rhs[0]
            q = jnp.maximum(jnp.dot(lhs, rhs, preferred_element_type=F32), 0.0)
            q = q * q * q
            for h in range(len(pair)):
                acc = acc + q[:, h * SLOTS:(h + 1) * SLOTS]
        total = jnp.sum(acc, axis=1, keepdims=True)
        col_ref[...] = jnp.where(lane == r, total, col_ref[...])
        return carry

    lax.fori_loop(0, 32, cell, 0)
    live = live_ref[...] < 32.0
    density = jnp.where(live, col_ref[...].T[0:32, :] / (SLOTS / 2.0), 0.0)
    safe = jnp.where(live, density, 1.0)
    press_ref[...] = jnp.where(live, (density - 1.0) / (safe * safe), 0.0)
    for a in range(2):
        for e in range(2):
            r = (a * 4 + 1 + e) * 4 + 1
            rho_ref[a, e] = density[r:r + 2, :]


def body_kernel(recv_ref, pos_ref, press_ref, force_ref, load_ref, flag_ref, list_ref, fa_ref, fb_ref, side_ref, shape_ref, react_ref, sums_ref, sem):
    slots = recv_ref.shape[0]
    copy = pltpu.make_async_copy(recv_ref, flag_ref, sem)
    copy.start()
    fa_ref[...] = jnp.zeros_like(fa_ref)
    fb_ref[...] = jnp.zeros_like(fb_ref)
    react_ref[...] = jnp.zeros_like(react_ref)
    sums_ref[...] = jnp.zeros_like(sums_ref)
    copy.wait()
    shapes = [flag_ref[:, m, :] for m in range(3)]
    for r, v in enumerate(own_rows(shapes) + shapes):
        fa_ref[r * slots:(r + 1) * slots, :] = v
    press = jnp.concatenate([press_ref[(a * 4 + 1 + e) * 4 + 1:(a * 4 + 1 + e) * 4 + 3, :] for a in range(2) for e in range(2)], axis=0)
    press = press * (24.0 / SLOTS)
    list_ref[...] = press
    sub = lax.broadcasted_iota(jnp.int32, (8, SLOTS), 0)
    lane = lax.broadcasted_iota(jnp.int32, (8, SLOTS), 1)
    coords = [pos_ref[m] for m in range(3)]

    def one(t, carry):
        extra = jnp.broadcast_to(flag_ref[t, 3:4, :], (8, SLOTS))
        used = jnp.max(jnp.where(lane == 32, extra, 0.0)) > 0.0

        @pl.when(used)
        def _():
            first = jnp.sum(jnp.where(lane == 24, extra, 0.0), axis=1, keepdims=True).astype(jnp.int32)
            k = jnp.bitwise_xor(sub, first)
            gaps = []
            for m in range(3):
                anchor = jnp.sum(jnp.where(lane == 8 * m + k, extra, 0.0), axis=1, keepdims=True)
                gaps.append(coords[m] - anchor)
            for r, v in enumerate(near_rows(gaps)):
                fb_ref[8 * r:8 * r + 8, :] = v
            for m in range(3):
                side_ref[8 * m:8 * m + 8, :] = -gaps[m]
            turned = fa_ref[pl.ds(t, ROWS, stride=slots), :].T
            lhs = turned.astype(BF16)
            for m in range(3):
                shape_ref[m] = jnp.broadcast_to(turned[:, 24 + m:25 + m], (SLOTS, SLOTS))
            sums = [jnp.zeros((8, SLOTS), F32) for _ in range(6)]
            for g in range(4):
                rhs = jnp.concatenate(
                    [fb_ref[pl.ds(c, ROWS, stride=8), :].astype(BF16) for c in (2 * g, 2 * g + 1)], axis=1
                )
                q = jnp.maximum(jnp.dot(lhs, rhs, preferred_element_type=F32), 0.0)
                q = q * q
                part = [[jnp.zeros((8, SLOTS), F32) for _ in range(4)] for _ in range(2)]
                for i in range(16):
                    arm = [shape_ref[m, 8 * i:8 * i + 8, :] for m in range(3)]
                    for h in range(2):
                        v = q[8 * i:8 * i + 8, h * SLOTS:(h + 1) * SLOTS]
                        part[h][0] = part[h][0] + v
                        for m in range(3):
                            part[h][1 + m] = part[h][1 + m] + v * arm[m]
                for h in range(2):
                    c = 2 * g + h
                    pr = list_ref[c:c + 1, :]
                    gap = [side_ref[8 * m + c:8 * m + c + 1, :] for m in range(3)]
                    push = [v * pr for v in part[h]]
                    for m in range(3):
                        total = push[1 + m] + gap[m] * push[0]
                        react_ref[m, c] = react_ref[m, c] + total
                        sums[m] = sums[m] + total
                        u, v = (m + 1) % 3, (m + 2) % 3
                        sums[3 + m] = sums[3 + m] + (push[1 + u] * gap[v] - push[1 + v] * gap[u])
            for r in range(6):
                sums_ref[t, r:r + 1, :] = jnp.sum(sums[r], axis=0, keepdims=True)

        return carry

    lax.fori_loop(0, slots, one, 0)
    for m in range(3):
        force_ref[m] = jnp.sum(react_ref[m], axis=1)
    load_ref[...] = jnp.sum(sums_ref[...], axis=2)


def accel_kernel(own_ref, near_ref, coord_ref, left_ref, mid_ref, right_ref, force_ref, out_ref, press_ref, col_ref, line_ref):
    press_ref[0:16, :] = left_ref[16:32, :]
    press_ref[16:48, :] = mid_ref[...]
    press_ref[48:64, :] = right_ref[0:16, :]
    turned = mid_ref[...].T
    for a in range(2):
        for e in range(2):
            for f in range(2):
                r = (a * 4 + 1 + e) * 4 + 1 + f
                col_ref[4 * a + 2 * e + f] = jnp.broadcast_to(turned[:, r:r + 1], (SLOTS, SLOTS))
    steps = [(dx, dy, dz) for dx in (-1, 0, 1) for dy in (-1, 0, 1) for dz in (-1, 0, 1)]
    lane = lax.broadcasted_iota(jnp.int32, (32, SLOTS), 1)

    def cell(c, carry):
        a, e, f = c // 4, c // 2 % 2, c % 2
        w = ((a + 1) * 6 + e + 2) * 6 + f + 2
        v = ((a + 1) * 4 + e + 1) * 4 + f + 1
        r = (a * 4 + 1 + e) * 4 + 1 + f
        for chunk in range(4):
            lhs = own_ref[r, chunk * 32:(chunk + 1) * 32, :]
            pi = col_ref[c, chunk * 32:(chunk + 1) * 32, :]
            acc = [jnp.zeros((32, SLOTS), F32) for _ in range(4)]
            for g in range(0, 27, 2):
                pair = steps[g:g + 2]
                rhs = [near_ref[w + (d[0] * 6 + d[1]) * 6 + d[2]] for d in pair]
                rhs = jnp.concatenate(rhs, axis=1) if len(rhs) == 2 else rhs[0]
                q = jnp.maximum(jnp.dot(lhs, rhs, preferred_element_type=F32), 0.0)
                q = q * q
                for h, d in enumerate(pair):
                    pj = press_ref[pl.ds(v + (d[0] * 4 + d[1]) * 4 + d[2], 1), :]
                    at = w + (d[0] * 6 + d[1]) * 6 + d[2]
                    weight = q[:, h * SLOTS:(h + 1) * SLOTS] * (pi + pj)
                    acc[0] = acc[0] + weight
                    for m in range(3):
                        acc[1 + m] = acc[1 + m] + weight * coord_ref[at, m:m + 1, :]
            line = jnp.zeros((32, SLOTS), F32)
            for s in range(4):
                line = jnp.where(lane == s, jnp.sum(acc[s], axis=1, keepdims=True), line)
            line_ref[chunk * 32:(chunk + 1) * 32, :] = line
        rows = line_ref[...].T
        live = coord_ref[w, 0:1, :] < 32.0
        for m in range(3):
            own = coord_ref[w, m:m + 1, :] * rows[0:1, :] - rows[1 + m:2 + m, :]
            own = jnp.where(live, own * (12.0 / SLOTS), 0.0)
            out_ref[m, a, e, pl.ds(f, 1), :] = own - force_ref[m, pl.ds(c, 1), :]
        return carry

    lax.fori_loop(0, 8, cell, 0)


def gather_kernel(slot_ref, got_ref, out_ref, pick_ref):
    bodies = out_ref.shape[1]
    pick_ref[...] = jnp.zeros_like(pick_ref)
    for b in range(bodies):
        pick_ref[b:b + 1, 0:8] = got_ref[pl.ds(slot_ref[b], 1), :]
    out_ref[...] = pick_ref[...].T[0:6, 0:bodies] / BODY_PARTS


def vmem():
    return pl.BlockSpec(memory_space=pltpu.VMEM)


def smem():
    return pl.BlockSpec(memory_space=pltpu.SMEM)


def params():
    return pltpu.CompilerParams(vmem_limit_bytes=56 << 20)


def both_ways(value, axis):
    count = lax.axis_size(axis)
    ups = [(i, i + 1) for i in range(count - 1)]
    downs = [(i + 1, i) for i in range(count - 1)]
    return lax.ppermute(value, axis, ups), lax.ppermute(value, axis, downs)


def shaped(*dims, dtype=F32):
    return jax.ShapeDtypeStruct(dims, dtype)


def local(fluid_pos, fluid_count, body_shape, body_anchor, body_dest, body_cell):
    groups = lax.axis_size("gx")
    bodies = body_shape.shape[1]
    slots = groups * CAPACITY
    pos, send, slot_of = pl.pallas_call(
        pack_kernel,
        out_shape=(shaped(3, 8, SLOTS), shaped(slots, 4, SLOTS), shaped(bodies, dtype=jnp.int32)),
        in_specs=[vmem(), smem(), vmem(), vmem(), smem(), vmem()],
        out_specs=(vmem(), vmem(), smem()),
        scratch_shapes=[pltpu.VMEM((bodies, SLOTS), F32), pltpu.SMEM((groups,), jnp.int32)],
        compiler_params=params(),
        name="pack",
    )(fluid_pos, fluid_count, body_shape, body_anchor, body_dest, body_cell)
    recv = lax.all_to_all(send.reshape(groups, CAPACITY, 4, SLOTS), "gx", 0, 0, tiled=True).reshape(slots, 4, SLOTS)
    low, high = both_ways(pos, "body")
    line = jnp.stack([low, pos, high])
    low, high = both_ways(line, "yz")
    sheet = jnp.stack([low, line, high]).reshape(9, 3, 8, SLOTS)
    left, right = both_ways(sheet, "gx")
    rho, press, near, coord, own = pl.pallas_call(
        density_kernel,
        out_shape=(
            shaped(2, 2, 2, SLOTS),
            shaped(32, SLOTS),
            shaped(144, ROWS, SLOTS, dtype=BF16),
            shaped(144, 8, SLOTS),
            shaped(32, SLOTS, ROWS, dtype=BF16),
        ),
        in_specs=[vmem()] * 3,
        out_specs=(vmem(),) * 5,
        scratch_shapes=[
            pltpu.VMEM((ROWS * 8, SLOTS), F32),
            pltpu.VMEM((9, ROWS * 8, SLOTS), F32),
            pltpu.VMEM((64, SLOTS), F32),
            pltpu.VMEM((32, SLOTS), F32),
            pltpu.VMEM((SLOTS, SLOTS), F32),
        ],
        compiler_params=params(),
        name="density",
    )(left, sheet, right)
    press_left, press_right = both_ways(press, "gx")
    force, load = pl.pallas_call(
        body_kernel,
        out_shape=(shaped(3, 8, SLOTS), shaped(slots, 8)),
        in_specs=[pl.BlockSpec(memory_space=pl.ANY), vmem(), vmem()],
        out_specs=(vmem(), vmem()),
        scratch_shapes=[
            pltpu.VMEM((slots, 4, SLOTS), F32),
            pltpu.VMEM((8, SLOTS), F32),
            pltpu.VMEM((ROWS * slots, SLOTS), F32),
            pltpu.VMEM((ROWS * 8, SLOTS), F32),
            pltpu.VMEM((24, SLOTS), F32),
            pltpu.VMEM((3, SLOTS, SLOTS), F32),
            pltpu.VMEM((3, 8, 8, SLOTS), F32),
            pltpu.VMEM((slots, 8, SLOTS), F32),
            pltpu.SemaphoreType.DMA,
        ],
        compiler_params=params(),
        name="bodies",
    )(recv, pos, press)
    got = lax.all_to_all(load.reshape(groups, CAPACITY, 8), "gx", 0, 0, tiled=True).reshape(slots, 8)
    accel = pl.pallas_call(
        accel_kernel,
        out_shape=shaped(3, 2, 2, 2, SLOTS),
        in_specs=[vmem()] * 7,
        out_specs=vmem(),
        scratch_shapes=[
            pltpu.VMEM((64, SLOTS), F32),
            pltpu.VMEM((8, SLOTS, SLOTS), F32),
            pltpu.VMEM((SLOTS, SLOTS), F32),
        ],
        compiler_params=params(),
        name="accel",
    )(own, near, coord, press_left, press, press_right, force)
    body_load = pl.pallas_call(
        gather_kernel,
        out_shape=shaped(6, bodies),
        in_specs=[smem(), vmem()],
        out_specs=vmem(),
        scratch_shapes=[pltpu.VMEM((SLOTS, SLOTS), F32)],
        compiler_params=params(),
        name="collect",
    )(slot_of, got)
    return rho, accel, body_load


def solution(mesh):
    in_specs = (
        P(None, "gx", "yz", "body", None),
        P("gx", "yz", "body"),
        P(None, ("gx", "yz", "body"), None),
        P(None, ("gx", "yz", "body"), None),
        P(("gx", "yz", "body"), None),
        P(("gx", "yz", "body"), None),
    )
    out_specs = (
        P("gx", "yz", "body", None),
        P(None, "gx", "yz", "body", None),
        P(None, ("gx", "yz", "body")),
    )
    return jax.shard_map(local, mesh=mesh, in_specs=in_specs, out_specs=out_specs, check_vma=False)
```

```python
import jax
import jax.numpy as jnp
from jax import lax
from jax.experimental import pallas as pl
from jax.experimental.pallas import tpu as pltpu
from jax.sharding import PartitionSpec as P

SLOTS = 128
BODY_PARTS = 128
CAPACITY = 3
FAR = 64.0
TOGETHER = 4
ROWS = 32
F32 = jnp.float32
BF16 = jnp.bfloat16


def split3(v):
    high = v.astype(BF16).astype(F32)
    rest = v - high
    mid = rest.astype(BF16).astype(F32)
    return high, mid, rest - mid


def near_rows(coords):
    rows = []
    norm = 0.0
    for v in coords:
        h, m, l = split3(v)
        rows += [h, m, h, l, h, m]
        norm = norm + v * v
    one = jnp.ones_like(norm)
    return rows + list(split3(-norm)) + [one, one, one]


def own_rows(coords):
    rows = []
    norm = 0.0
    for v in coords:
        h, m, l = split3(2.0 * v)
        rows += [h, h, m, h, l, m]
        norm = norm + v * v
    one = jnp.ones_like(norm)
    return rows + [one, one, one] + list(split3(1.0 - norm))


def place_kernel(pos_ref, count_ref, out_ref):
    lane = lax.broadcasted_iota(jnp.int32, (2, SLOTS), 1)
    row = lax.broadcasted_iota(jnp.int32, (2, SLOTS), 0)
    for a in range(2):
        for e in range(2):
            count = jnp.where(row == 0, count_ref[a, e, 0], count_ref[a, e, 1])
            live = lane < count
            base = 4 * a + 2 * e
            out_ref[0, base:base + 2, :] = jnp.where(live, pos_ref[0, a, e], FAR)
            out_ref[1, base:base + 2, :] = pos_ref[1, a, e]
            out_ref[2, base:base + 2, :] = pos_ref[2, a, e]


def pack_kernel(shape_ref, anchor_ref, dest_ref, cell_ref, send_ref, slot_ref, extra_ref, tally_ref):
    bodies = shape_ref.shape[1]
    groups = tally_ref.shape[0]
    send_ref[...] = jnp.zeros_like(send_ref)
    extra_ref[...] = jnp.zeros_like(extra_ref)
    first = cell_ref[0:1, :]
    for m in range(3):
        rows = [anchor_ref[m, k:k + 1, :] for k in range(8)]
        for bit in (1, 2, 4):
            flip = (first & bit) > 0
            rows = [jnp.where(flip, rows[k ^ bit], rows[k]) for k in range(8)]
        for k in range(8):
            extra_ref[8 * m + k:8 * m + k + 1, 0:bodies] = rows[k]
    extra_ref[24:32, :] = jnp.ones((8, SLOTS), F32)
    extra_ref[...] = extra_ref[...].T
    for g in range(groups):
        tally_ref[g] = 0
    for b in range(bodies):
        dest = dest_ref[0, b]
        rank = tally_ref[dest]
        tally_ref[dest] = rank + 1
        slot_ref[b] = dest * 8 + rank
        slot = dest * CAPACITY + rank
        send_ref[slot, 0:3, :] = shape_ref[:, b, :]
        send_ref[slot, 3:4, :] = extra_ref[b:b + 1, :]


def density_kernel(left_ref, mid_ref, right_ref, rho_ref, press_ref, near_out, coord_out, own_out, near_ref, coord_ref, own_ref, fb_ref, fa_ref, fr_ref, live_ref, col_ref):
    index = [lax.axis_index(n) for n in ("gx", "yz", "body")]
    size = [lax.axis_size(n) for n in ("gx", "yz", "body")]
    sub = lax.broadcasted_iota(jnp.int32, (8, SLOTS), 0)
    part = [sub // 4, sub // 2 % 2, sub % 2]
    fb_ref[...] = jnp.zeros_like(fb_ref)
    fa_ref[...] = jnp.zeros_like(fa_ref)
    fr_ref[...] = jnp.zeros_like(fr_ref)

    def block(t, carry):
        by = t // 3
        bz = t % 3
        ny = index[1] + by - 1
        nz = index[2] + bz - 1
        inside = (ny >= 0) & (ny < size[1]) & (nz >= 0) & (nz < size[2])
        off_y = (part[1] + 2 * by - 3).astype(F32)
        off_z = (part[2] + 2 * bz - 3).astype(F32)
        for kind in range(2):
            if kind == 0:
                raw = [mid_ref[t, m] for m in range(3)]
                wx = part[0] + 1
                ok = jnp.full((8, SLOTS), inside)
            else:
                raw = [jnp.where(sub >= 4, left_ref[t, m], right_ref[t, m]) for m in range(3)]
                wx = 3 - 3 * part[0]
                ok = jnp.where(sub >= 4, index[0], size[0] - 1 - index[0]) > 0
                ok = ok & inside
            coords = [
                jnp.where(ok, raw[0], FAR) + (wx - 2).astype(F32),
                raw[1] + off_y,
                raw[2] + off_z,
            ]
            for r, v in enumerate(near_rows(coords)):
                fb_ref[8 * r:8 * r + 8, :] = v
            for m in range(3):
                fr_ref[8 * m:8 * m + 8, :] = coords[m]
            if kind == 0:
                for r, v in enumerate(own_rows(coords)):
                    fa_ref[t, 8 * r:8 * r + 8, :] = v
            for c in range(8):
                a, e, f = c // 4, c // 2 % 2, c % 2
                at_x = 1 + a if kind == 0 else 3 - 3 * a
                w = (at_x * 6 + 2 * by + e) * 6 + 2 * bz + f
                near_ref[w] = fb_ref[pl.ds(c, ROWS, stride=8), :].astype(BF16)
                coord_ref[w] = fr_ref[pl.ds(c, 8, stride=8), :]
        return carry

    lax.fori_loop(0, 9, block, 0)

    def turn(r, carry):
        wy = r // 4 % 4 + 1
        wz = r % 4 + 1
        t = wy // 2 * 3 + wz // 2
        c = r // 16 * 4 + wy % 2 * 2 + wz % 2
        own_ref[r] = fa_ref[t, pl.ds(c, ROWS, stride=8), :].T.astype(BF16)
        w = ((r // 16 + 1) * 6 + wy) * 6 + wz
        live_ref[pl.ds(r, 1), :] = coord_ref[w, 0:1, :]
        return carry

    lax.fori_loop(0, 32, turn, 0, unroll=16)
    for i in range(16):
        w = ((i // 4) * 6 + i % 4 + 1) * 6 + 1
        near_out[4 * i:4 * i + 4] = near_ref[w:w + 4]
        coord_out[4 * i:4 * i + 4] = coord_ref[w:w + 4]
    for a in range(2):
        for e in range(2):
            r = (a * 4 + 1 + e) * 4 + 1
            own_out[4 * a + 2 * e:4 * a + 2 * e + 2] = own_ref[r:r + 2]
    col_ref[...] = jnp.zeros_like(col_ref)
    lane = lax.broadcasted_iota(jnp.int32, (SLOTS, SLOTS), 1)

    def cell(r, carry):
        w = ((r // 16 + 1) * 6 + r // 4 % 4 + 1) * 6 + r % 4 + 1
        lhs = own_ref[r]
        acc = jnp.zeros((SLOTS, SLOTS), F32)
        steps = [(dx * 6 + dy) * 6 + dz for dx in (-1, 0, 1) for dy in (-1, 0, 1) for dz in (-1, 0, 1)]
        for g in range(0, 27, 2):
            pair = steps[g:g + 2]
            rhs = [near_ref[w + s] for s in pair]
            rhs = jnp.concatenate(rhs, axis=1) if len(rhs) == 2 else rhs[0]
            q = jnp.maximum(jnp.dot(lhs, rhs, preferred_element_type=F32), 0.0)
            q = q * q * q
            for h in range(len(pair)):
                acc = acc + q[:, h * SLOTS:(h + 1) * SLOTS]
        total = jnp.sum(acc, axis=1, keepdims=True)
        col_ref[...] = jnp.where(lane == r, total, col_ref[...])
        return carry

    lax.fori_loop(0, 32, cell, 0, unroll=8)
    live = live_ref[...] < 32.0
    density = jnp.where(live, col_ref[...].T[0:32, :] / (SLOTS / 2.0), 0.0)
    safe = jnp.where(live, density, 1.0)
    press_ref[...] = jnp.where(live, (density - 1.0) / (safe * safe), 0.0)
    for a in range(2):
        for e in range(2):
            r = (a * 4 + 1 + e) * 4 + 1
            rho_ref[a, e] = density[r:r + 2, :]


def body_kernel(recv_ref, pos_ref, press_ref, force_ref, load_ref, list_ref, fa_ref, used_ref, anchor_ref, near_ref, side_ref, arm_ref, react_ref, sums_ref, pick_ref, order_ref, sem):
    slots = recv_ref.shape[0]
    blank = jnp.zeros((8, SLOTS), F32)
    near_ref[...] = jnp.zeros_like(near_ref)
    react_ref[...] = jnp.zeros_like(react_ref)
    sums_ref[...] = jnp.zeros_like(sums_ref)
    fa_ref[27 * slots:, :] = jnp.zeros((5 * slots, SLOTS), F32)
    extras = jnp.concatenate([recv_ref[:, 3, :], jnp.zeros((SLOTS - slots, SLOTS), F32)], axis=0).T
    used_ref[...] = extras[24:32, :]
    down = pltpu.make_async_copy(used_ref, pick_ref, sem)
    down.start()
    shapes = [recv_ref[:, m, :] for m in range(3)]
    for r, v in enumerate(own_rows(shapes) + shapes):
        fa_ref[r * slots:(r + 1) * slots, :] = v
    for t in range(slots):
        for m in range(3):
            anchor_ref[t, 8 * m:8 * m + 8, :] = jnp.broadcast_to(extras[8 * m:8 * m + 8, t:t + 1], (8, SLOTS))
    press = jnp.concatenate([press_ref[(a * 4 + 1 + e) * 4 + 1:(a * 4 + 1 + e) * 4 + 3, :] for a in range(2) for e in range(2)], axis=0)
    list_ref[...] = press * (24.0 / SLOTS)
    down.wait()
    busy = jnp.int32(0)
    spare = jnp.int32(0)
    for t in range(slots):
        order_ref[busy] = t
        flag = pick_ref[0, t] > 0.0
        spare = jnp.where(flag, spare, t)
        busy = busy + flag.astype(jnp.int32)
    for n in range(TOGETHER - 1):
        order_ref[busy + n] = spare
    coords = [pos_ref[m] for m in range(3)]

    def one(t, n):
        gaps = [coords[m] - anchor_ref[t, 8 * m:8 * m + 8, :] for m in range(3)]
        for r, v in enumerate(near_rows(gaps)):
            near_ref[n, 8 * r:8 * r + 8, :] = v
        for m in range(3):
            side_ref[n, 8 * m:8 * m + 8, :] = -gaps[m]
        side_ref[n, 24:32, :] = list_ref[...] * pick_ref[0, t]
        turned = fa_ref[pl.ds(t, ROWS, stride=slots), :].T
        lhs = turned.astype(BF16)
        for m in range(3):
            arm_ref[n, m] = jnp.broadcast_to(turned[:, 24 + m:25 + m], (SLOTS, SLOTS))
        sums = [blank] * 6
        reacts = []
        for g in range(4):
            rhs = jnp.concatenate(
                [near_ref[n, pl.ds(c, ROWS, stride=8), :].astype(BF16) for c in (2 * g, 2 * g + 1)], axis=1
            )
            q = jnp.maximum(jnp.dot(lhs, rhs, preferred_element_type=F32), 0.0)
            q = q * q
            part = [[blank] * 4 for _ in range(2)]
            for i in range(16):
                arm = [arm_ref[n, m, 8 * i:8 * i + 8, :] for m in range(3)]
                for h in range(2):
                    v = q[8 * i:8 * i + 8, h * SLOTS:(h + 1) * SLOTS]
                    part[h][0] = part[h][0] + v
                    for m in range(3):
                        part[h][1 + m] = part[h][1 + m] + v * arm[m]
            for h in range(2):
                c = 2 * g + h
                pr = side_ref[n, 24 + c:25 + c, :]
                gap = [side_ref[n, 8 * m + c:8 * m + c + 1, :] for m in range(3)]
                push = [v * pr for v in part[h]]
                for m in range(3):
                    total = push[1 + m] + gap[m] * push[0]
                    reacts.append(total)
                    sums[m] = sums[m] + total
                    u, v = (m + 1) % 3, (m + 2) % 3
                    sums[3 + m] = sums[3 + m] + (push[1 + u] * gap[v] - push[1 + v] * gap[u])
        return reacts, sums

    def step(i, carry):
        picked = [order_ref[TOGETHER * i + n] for n in range(TOGETHER)]
        done = [one(t, n) for n, t in enumerate(picked)]
        for r in range(24):
            react_ref[r] = react_ref[r] + sum(d[0][r] for d in done)
        for t, d in zip(picked, done):
            for r in range(6):
                sums_ref[t, r:r + 1, :] = jnp.sum(d[1][r], axis=0, keepdims=True)
        return carry

    lax.fori_loop(0, (busy + TOGETHER - 1) // TOGETHER, step, 0)
    for r in range(24):
        force_ref[r % 3, r // 3:r // 3 + 1, :] = jnp.sum(react_ref[r], axis=0, keepdims=True)
    total = jnp.sum(sums_ref[...], axis=2)
    load_ref[...] = jnp.zeros_like(load_ref)
    for g in range(slots // CAPACITY):
        load_ref[g, 0:CAPACITY, 0:8] = total[CAPACITY * g:CAPACITY * g + CAPACITY, :]


def accel_kernel(own_ref, near_ref, coord_ref, left_ref, mid_ref, right_ref, force_ref, out_ref, press_ref, col_ref, line_ref):
    press_ref[0:16, :] = left_ref[16:32, :]
    press_ref[16:48, :] = mid_ref[...]
    press_ref[48:64, :] = right_ref[0:16, :]
    turned = mid_ref[...].T
    for a in range(2):
        for e in range(2):
            for f in range(2):
                r = (a * 4 + 1 + e) * 4 + 1 + f
                col_ref[4 * a + 2 * e + f] = jnp.broadcast_to(turned[:, r:r + 1], (SLOTS, SLOTS))
    steps = [(dx * 4 + dy) * 4 + dz for dx in (-1, 0, 1) for dy in (-1, 0, 1) for dz in (-1, 0, 1)]
    lane = lax.broadcasted_iota(jnp.int32, (32, SLOTS), 1)

    def cell(c, carry):
        a, e, f = c // 4, c // 2 % 2, c % 2
        w = ((a + 1) * 4 + e + 1) * 4 + f + 1

        def chunk(n):
            lhs = own_ref[c, n * 32:(n + 1) * 32, :]
            pi = col_ref[c, n * 32:(n + 1) * 32, :]
            acc = [jnp.zeros((32, SLOTS), F32) for _ in range(4)]
            for g in range(0, 27, 2):
                pair = steps[g:g + 2]
                rhs = [near_ref[w + s] for s in pair]
                rhs = jnp.concatenate(rhs, axis=1) if len(rhs) == 2 else rhs[0]
                q = jnp.maximum(jnp.dot(lhs, rhs, preferred_element_type=F32), 0.0)
                q = q * q
                for h, s in enumerate(pair):
                    weight = q[:, h * SLOTS:(h + 1) * SLOTS] * (pi + press_ref[pl.ds(w + s, 1), :])
                    acc[0] = acc[0] + weight
                    for m in range(3):
                        acc[1 + m] = acc[1 + m] + weight * coord_ref[w + s, m:m + 1, :]
            line = jnp.zeros((32, SLOTS), F32)
            for s in range(4):
                line = jnp.where(lane == s, jnp.sum(acc[s], axis=1, keepdims=True), line)
            line_ref[n * 32:(n + 1) * 32, :] = line

        for n in range(4):
            chunk(n)
        rows = line_ref[...].T
        live = coord_ref[w, 0:1, :] < 32.0
        for m in range(3):
            own = coord_ref[w, m:m + 1, :] * rows[0:1, :] - rows[1 + m:2 + m, :]
            own = jnp.where(live, own * (12.0 / SLOTS), 0.0)
            out_ref[m, a, e, pl.ds(f, 1), :] = own - force_ref[m, pl.ds(c, 1), :]
        return carry

    lax.fori_loop(0, 8, cell, 0, unroll=4)


def gather_kernel(slot_ref, got_ref, out_ref, pick_ref):
    bodies = out_ref.shape[1]
    pick_ref[...] = jnp.zeros_like(pick_ref)
    for b in range(bodies):
        place = slot_ref[b]
        pick_ref[b:b + 1, :] = got_ref[place // 8, pl.ds(place % 8, 1), :]
    out_ref[...] = pick_ref[...].T[0:6, 0:bodies] / BODY_PARTS


def vmem():
    return pl.BlockSpec(memory_space=pltpu.VMEM)


def smem():
    return pl.BlockSpec(memory_space=pltpu.SMEM)


def params():
    return pltpu.CompilerParams(vmem_limit_bytes=56 << 20)


def held(*values):
    return [pltpu.with_memory_space_constraint(v, pltpu.VMEM) for v in values]


def inner(*dims, dtype=F32):
    return pltpu.VMEM(dims, dtype)


def cost(giga):
    return pl.CostEstimate(flops=giga * 10**9 // 10, transcendentals=0, bytes_accessed=1 << 18)


def both_ways(value, axis):
    count = lax.axis_size(axis)
    ups = [(i, i + 1) for i in range(count - 1)]
    downs = [(i + 1, i) for i in range(count - 1)]
    return lax.ppermute(value, axis, ups), lax.ppermute(value, axis, downs)


def shaped(*dims, dtype=F32):
    return jax.ShapeDtypeStruct(dims, dtype)


def local(fluid_pos, fluid_count, body_shape, body_anchor, body_dest, body_cell):
    groups = lax.axis_size("gx")
    bodies = body_shape.shape[1]
    slots = groups * CAPACITY
    pos = pl.pallas_call(
        place_kernel,
        out_shape=inner(3, 8, SLOTS),
        in_specs=[vmem(), smem()],
        out_specs=vmem(),
        compiler_params=params(),
        name="place",
    )(fluid_pos, fluid_count)
    send, slot_of = pl.pallas_call(
        pack_kernel,
        out_shape=(inner(slots, 4, SLOTS), shaped(bodies, dtype=jnp.int32)),
        in_specs=[vmem(), vmem(), smem(), vmem()],
        out_specs=(vmem(), smem()),
        scratch_shapes=[pltpu.VMEM((SLOTS, SLOTS), F32), pltpu.SMEM((groups,), jnp.int32)],
        compiler_params=params(),
        cost_estimate=cost(4),
        name="pack",
    )(body_shape, jnp.swapaxes(body_anchor, 1, 2), body_dest.reshape(1, bodies), body_cell.T)
    low, high = both_ways(pos, "body")
    low, high, send = lax.optimization_barrier((low, high, send))
    recv = lax.all_to_all(send.reshape(groups, CAPACITY, 4, SLOTS), "gx", 0, 0, tiled=True).reshape(slots, 4, SLOTS)
    line = jnp.stack([low, pos, high])
    low, high = both_ways(line, "yz")
    sheet = jnp.stack([low, line, high]).reshape(9, 3, 8, SLOTS)
    left, right = both_ways(sheet, "gx")
    rho, press, near, coord, own = pl.pallas_call(
        density_kernel,
        out_shape=(
            shaped(2, 2, 2, SLOTS),
            inner(32, SLOTS),
            inner(64, ROWS, SLOTS, dtype=BF16),
            inner(64, 8, SLOTS),
            inner(8, SLOTS, ROWS, dtype=BF16),
        ),
        in_specs=[vmem()] * 3,
        out_specs=(vmem(),) * 5,
        scratch_shapes=[
            pltpu.VMEM((144, ROWS, SLOTS), BF16),
            pltpu.VMEM((144, 8, SLOTS), F32),
            pltpu.VMEM((32, SLOTS, ROWS), BF16),
            pltpu.VMEM((ROWS * 8, SLOTS), F32),
            pltpu.VMEM((9, ROWS * 8, SLOTS), F32),
            pltpu.VMEM((64, SLOTS), F32),
            pltpu.VMEM((32, SLOTS), F32),
            pltpu.VMEM((SLOTS, SLOTS), F32),
        ],
        compiler_params=params(),
        cost_estimate=cost(60),
        name="density",
    )(*held(left, sheet, right))
    press_left, press_right = both_ways(press, "gx")
    force, load = pl.pallas_call(
        body_kernel,
        out_shape=(inner(3, 8, SLOTS), inner(groups, 8, SLOTS)),
        in_specs=[vmem(), vmem(), vmem()],
        out_specs=(vmem(), vmem()),
        scratch_shapes=[
            pltpu.VMEM((8, SLOTS), F32),
            pltpu.VMEM((ROWS * slots, SLOTS), F32),
            pltpu.VMEM((8, SLOTS), F32),
            pltpu.VMEM((slots, 24, SLOTS), F32),
            pltpu.VMEM((TOGETHER, ROWS * 8, SLOTS), F32),
            pltpu.VMEM((TOGETHER, 32, SLOTS), F32),
            pltpu.VMEM((TOGETHER, 3, SLOTS, SLOTS), F32),
            pltpu.VMEM((24, 8, SLOTS), F32),
            pltpu.VMEM((slots, 8, SLOTS), F32),
            pltpu.SMEM((8, SLOTS), F32),
            pltpu.SMEM((slots + TOGETHER,), jnp.int32),
            pltpu.SemaphoreType.DMA,
        ],
        compiler_params=params(),
        cost_estimate=cost(60),
        name="bodies",
    )(*held(recv, pos, press))
    got = lax.all_to_all(load, "gx", 0, 0, tiled=True)
    accel = pl.pallas_call(
        accel_kernel,
        out_shape=shaped(3, 2, 2, 2, SLOTS),
        in_specs=[vmem()] * 7,
        out_specs=vmem(),
        scratch_shapes=[
            pltpu.VMEM((64, SLOTS), F32),
            pltpu.VMEM((8, SLOTS, SLOTS), F32),
            pltpu.VMEM((SLOTS, SLOTS), F32),
        ],
        compiler_params=params(),
        cost_estimate=cost(40),
        name="accel",
    )(*held(own, near, coord, press_left, press, press_right, force))
    body_load = pl.pallas_call(
        gather_kernel,
        out_shape=shaped(6, bodies),
        in_specs=[smem(), vmem()],
        out_specs=vmem(),
        scratch_shapes=[pltpu.VMEM((SLOTS, SLOTS), F32)],
        compiler_params=params(),
        cost_estimate=cost(1),
        name="collect",
    )(slot_of, *held(got))
    return rho, accel, body_load


def solution(mesh):
    in_specs = (
        P(None, "gx", "yz", "body", None),
        P("gx", "yz", "body"),
        P(None, ("gx", "yz", "body"), None),
        P(None, ("gx", "yz", "body"), None),
        P(("gx", "yz", "body"), None),
        P(("gx", "yz", "body"), None),
    )
    out_specs = (
        P("gx", "yz", "body", None),
        P(None, "gx", "yz", "body", None),
        P(None, ("gx", "yz", "body")),
    )
    return jax.shard_map(local, mesh=mesh, in_specs=in_specs, out_specs=out_specs, check_vma=False)
```

```python
import jax
import jax.numpy as jnp
from jax import lax
from jax.experimental import pallas as pl
from jax.experimental.pallas import tpu as pltpu
from jax.sharding import PartitionSpec as P

SLOTS = 128
BODY_PARTS = 128
CAPACITY = 3
FAR = 64.0
TOGETHER = 4
ROWS = 32
F32 = jnp.float32
BF16 = jnp.bfloat16


def split3(v):
    high = v.astype(BF16).astype(F32)
    rest = v - high
    mid = rest.astype(BF16).astype(F32)
    return high, mid, rest - mid


def near_rows(coords):
    rows = []
    norm = 0.0
    for v in coords:
        h, m, l = split3(v)
        rows += [h, m, h, l, h, m]
        norm = norm + v * v
    one = jnp.ones_like(norm)
    return rows + list(split3(-norm)) + [one, one, one]


def own_rows(coords):
    rows = []
    norm = 0.0
    for v in coords:
        h, m, l = split3(2.0 * v)
        rows += [h, h, m, h, l, m]
        norm = norm + v * v
    one = jnp.ones_like(norm)
    return rows + [one, one, one] + list(split3(1.0 - norm))


def place_kernel(pos_ref, count_ref, out_ref):
    lane = lax.broadcasted_iota(jnp.int32, (2, SLOTS), 1)
    row = lax.broadcasted_iota(jnp.int32, (2, SLOTS), 0)
    for a in range(2):
        for e in range(2):
            count = jnp.where(row == 0, count_ref[a, e, 0], count_ref[a, e, 1])
            live = lane < count
            base = 4 * a + 2 * e
            out_ref[0, base:base + 2, :] = jnp.where(live, pos_ref[0, a, e], FAR)
            out_ref[1, base:base + 2, :] = pos_ref[1, a, e]
            out_ref[2, base:base + 2, :] = pos_ref[2, a, e]


def pack_kernel(shape_ref, anchor_ref, dest_ref, cell_ref, send_ref, slot_ref, extra_ref, tally_ref):
    bodies = shape_ref.shape[1]
    groups = tally_ref.shape[0]
    send_ref[...] = jnp.zeros_like(send_ref)
    extra_ref[...] = jnp.zeros_like(extra_ref)
    first = cell_ref[0:1, :]
    for m in range(3):
        rows = [anchor_ref[m, k:k + 1, :] for k in range(8)]
        for bit in (1, 2, 4):
            flip = (first & bit) > 0
            rows = [jnp.where(flip, rows[k ^ bit], rows[k]) for k in range(8)]
        for k in range(8):
            extra_ref[8 * m + k:8 * m + k + 1, 0:bodies] = rows[k]
    extra_ref[24:32, :] = jnp.ones((8, SLOTS), F32)
    extra_ref[...] = extra_ref[...].T
    for g in range(groups):
        tally_ref[g] = 0
    for b in range(bodies):
        dest = dest_ref[0, b]
        rank = tally_ref[dest]
        tally_ref[dest] = rank + 1
        slot_ref[b] = dest * 8 + rank
        slot = dest * CAPACITY + rank
        send_ref[slot, 0:3, :] = shape_ref[:, b, :]
        send_ref[slot, 3:4, :] = extra_ref[b:b + 1, :]


def inside_of(by, bz):
    ny = lax.axis_index("yz") + by - 1
    nz = lax.axis_index("body") + bz - 1
    return (ny >= 0) & (ny < lax.axis_size("yz")) & (nz >= 0) & (nz < lax.axis_size("body"))


def block_of(t):
    by = jnp.where(lax.axis_index("yz") % 2 == 1, t // 3, 2 - t // 3)
    bz = jnp.where(lax.axis_index("body") % 2 == 1, t % 3, 2 - t % 3)
    return by, bz


def centre_kernel(mid_ref, near_ref, coord_ref, own_ref, live_ref, col_ref, fb_ref, fa_ref, fr_ref):
    sub = lax.broadcasted_iota(jnp.int32, (8, SLOTS), 0)
    part = [sub // 4, sub // 2 % 2, sub % 2]
    for ref in (fb_ref, fr_ref):
        ref[...] = jnp.zeros_like(ref)
    fa_ref[:, 192:, :] = jnp.zeros((9, 64, SLOTS), F32)

    def block(t, carry):
        by, bz = block_of(t)
        inside = jnp.full((8, SLOTS), inside_of(by, bz))
        coords = [
            jnp.where(inside, mid_ref[t, 0], FAR) + (part[0] - 1).astype(F32),
            mid_ref[t, 1] + (part[1] + 2 * by - 3).astype(F32),
            mid_ref[t, 2] + (part[2] + 2 * bz - 3).astype(F32),
        ]
        for r, v in enumerate(near_rows(coords)):
            fb_ref[8 * r:8 * r + 8, :] = v
        for m in range(3):
            fr_ref[8 * m:8 * m + 8, :] = coords[m]
        for r, v in enumerate(own_rows(coords)):
            fa_ref[by * 3 + bz, 8 * r:8 * r + 8, :] = v
        for c in range(8):
            a, e, f = c // 4, c // 2 % 2, c % 2
            w = (a * 6 + 2 * by + e) * 6 + 2 * bz + f
            near_ref[w] = fb_ref[pl.ds(c, ROWS, stride=8), :].astype(BF16)
            coord_ref[w] = fr_ref[pl.ds(c, 8, stride=8), :]
        return carry

    lax.fori_loop(0, 9, block, 0)

    def turn(r, carry):
        wy = r // 4 % 4 + 1
        wz = r % 4 + 1
        t = wy // 2 * 3 + wz // 2
        c = r // 16 * 4 + wy % 2 * 2 + wz % 2
        own_ref[r] = fa_ref[t, pl.ds(c, ROWS, stride=8), :].T.astype(BF16)
        live_ref[pl.ds(r, 1), :] = coord_ref[(r // 16 * 6 + wy) * 6 + wz, 0:1, :]
        return carry

    lax.fori_loop(0, 32, turn, 0, unroll=16)
    col_ref[...] = jnp.zeros_like(col_ref)
    steps = [36 * x + 6 * dy + dz for x in (0, 1) for dy in (-1, 0, 1) for dz in (-1, 0, 1)]

    def cell(r, carry):
        add_tiles(col_ref, r, own_ref, near_ref, (r // 4 % 4 + 1) * 6 + r % 4 + 1, steps)
        return carry

    lax.fori_loop(0, 32, cell, 0, unroll=8)


def add_tiles(col_ref, r, own_ref, near_ref, base, steps):
    lane = lax.broadcasted_iota(jnp.int32, (SLOTS, SLOTS), 1)
    lhs = own_ref[r]
    acc = jnp.zeros((SLOTS, SLOTS), F32)
    for g in range(0, len(steps), 2):
        rhs = [near_ref[base + s] for s in steps[g:g + 2]]
        q = jnp.concatenate(rhs, axis=1) if len(rhs) == 2 else rhs[0]
        q = jnp.maximum(jnp.dot(lhs, q, preferred_element_type=F32), 0.0)
        q = q * q * q
        for h in range(len(rhs)):
            acc = acc + q[:, h * SLOTS:(h + 1) * SLOTS]
    total = jnp.sum(acc, axis=1, keepdims=True)
    col_ref[...] = jnp.where(lane == r, col_ref[...] + total, col_ref[...])


def side_kernel(left_ref, right_ref, near_mid, coord_mid, own_ref, live_ref, part_ref, rho_ref, press_ref, near_out, coord_out, own_out, near_ref, coord_ref, fb_ref, fr_ref, col_ref):
    sub = lax.broadcasted_iota(jnp.int32, (8, SLOTS), 0)
    part = [sub // 4, sub // 2 % 2, sub % 2]
    for ref in (fb_ref, fr_ref):
        ref[...] = jnp.zeros_like(ref)
    gx = lax.axis_index("gx")
    beside = jnp.where(sub >= 4, gx, lax.axis_size("gx") - 1 - gx) > 0

    def block(t, carry):
        by, bz = block_of(t)
        inside = jnp.full((8, SLOTS), inside_of(by, bz)) & beside
        raw = [jnp.where(sub >= 4, left_ref[t, m], right_ref[t, m]) for m in range(3)]
        coords = [
            jnp.where(inside, raw[0], FAR) + (1 - 3 * part[0]).astype(F32),
            raw[1] + (part[1] + 2 * by - 3).astype(F32),
            raw[2] + (part[2] + 2 * bz - 3).astype(F32),
        ]
        for r, v in enumerate(near_rows(coords)):
            fb_ref[8 * r:8 * r + 8, :] = v
        for m in range(3):
            fr_ref[8 * m:8 * m + 8, :] = coords[m]
        for c in range(8):
            a, e, f = c // 4, c // 2 % 2, c % 2
            w = ((1 - a) * 6 + 2 * by + e) * 6 + 2 * bz + f
            near_ref[w] = fb_ref[pl.ds(c, ROWS, stride=8), :].astype(BF16)
            coord_ref[w] = fr_ref[pl.ds(c, 8, stride=8), :]
        return carry

    lax.fori_loop(0, 9, block, 0)
    col_ref[...] = part_ref[...]
    steps = [6 * dy + dz for dy in (-1, 0, 1) for dz in (-1, 0, 1)]

    def cell(r, carry):
        add_tiles(col_ref, r, own_ref, near_ref, r // 16 * 36 + (r // 4 % 4 + 1) * 6 + r % 4 + 1, steps)
        return carry

    lax.fori_loop(0, 32, cell, 0, unroll=8)
    for i in range(16):
        x, y = i // 4, i % 4
        w = (y + 1) * 6 + 1
        near, coord = ((near_ref, coord_ref) if x in (0, 3) else (near_mid, coord_mid))
        w = w + (36 if x >= 2 else 0)
        near_out[4 * i:4 * i + 4] = near[w:w + 4]
        coord_out[4 * i:4 * i + 4] = coord[w:w + 4]
    for a in range(2):
        for e in range(2):
            r = (a * 4 + 1 + e) * 4 + 1
            own_out[4 * a + 2 * e:4 * a + 2 * e + 2] = own_ref[r:r + 2]
    live = live_ref[...] < 32.0
    density = jnp.where(live, col_ref[...].T[0:32, :] / (SLOTS / 2.0), 0.0)
    safe = jnp.where(live, density, 1.0)
    press_ref[...] = jnp.where(live, (density - 1.0) / (safe * safe), 0.0)
    for a in range(2):
        for e in range(2):
            r = (a * 4 + 1 + e) * 4 + 1
            rho_ref[a, e] = density[r:r + 2, :]


def body_kernel(recv_ref, pos_ref, press_ref, force_ref, load_ref, list_ref, fa_ref, used_ref, anchor_ref, near_ref, side_ref, arm_ref, react_ref, sums_ref, pick_ref, order_ref, sem):
    slots = recv_ref.shape[0]
    blank = jnp.zeros((8, SLOTS), F32)
    near_ref[...] = jnp.zeros_like(near_ref)
    react_ref[...] = jnp.zeros_like(react_ref)
    sums_ref[...] = jnp.zeros_like(sums_ref)
    fa_ref[27 * slots:, :] = jnp.zeros((5 * slots, SLOTS), F32)
    extras = jnp.concatenate([recv_ref[:, 3, :], jnp.zeros((SLOTS - slots, SLOTS), F32)], axis=0).T
    used_ref[...] = extras[24:32, :]
    down = pltpu.make_async_copy(used_ref, pick_ref, sem)
    down.start()
    shapes = [recv_ref[:, m, :] for m in range(3)]
    for r, v in enumerate(own_rows(shapes) + shapes):
        fa_ref[r * slots:(r + 1) * slots, :] = v
    for t in range(slots):
        for m in range(3):
            anchor_ref[t, 8 * m:8 * m + 8, :] = jnp.broadcast_to(extras[8 * m:8 * m + 8, t:t + 1], (8, SLOTS))
    press = jnp.concatenate([press_ref[(a * 4 + 1 + e) * 4 + 1:(a * 4 + 1 + e) * 4 + 3, :] for a in range(2) for e in range(2)], axis=0)
    list_ref[...] = press * (24.0 / SLOTS)
    down.wait()
    busy = jnp.int32(0)
    spare = jnp.int32(0)
    for t in range(slots):
        order_ref[busy] = t
        flag = pick_ref[0, t] > 0.0
        spare = jnp.where(flag, spare, t)
        busy = busy + flag.astype(jnp.int32)
    for n in range(TOGETHER - 1):
        order_ref[busy + n] = spare
    coords = [pos_ref[m] for m in range(3)]

    def one(t, n):
        gaps = [coords[m] - anchor_ref[t, 8 * m:8 * m + 8, :] for m in range(3)]
        for r, v in enumerate(near_rows(gaps)):
            near_ref[n, 8 * r:8 * r + 8, :] = v
        for m in range(3):
            side_ref[n, 8 * m:8 * m + 8, :] = -gaps[m]
        side_ref[n, 24:32, :] = list_ref[...] * pick_ref[0, t]
        turned = fa_ref[pl.ds(t, ROWS, stride=slots), :].T
        lhs = turned.astype(BF16)
        for m in range(3):
            arm_ref[n, m] = jnp.broadcast_to(turned[:, 24 + m:25 + m], (SLOTS, SLOTS))
        sums = [blank] * 6
        reacts = []
        for g in range(4):
            rhs = jnp.concatenate(
                [near_ref[n, pl.ds(c, ROWS, stride=8), :].astype(BF16) for c in (2 * g, 2 * g + 1)], axis=1
            )
            q = jnp.maximum(jnp.dot(lhs, rhs, preferred_element_type=F32), 0.0)
            q = q * q
            part = [[blank] * 4 for _ in range(2)]
            for i in range(16):
                arm = [arm_ref[n, m, 8 * i:8 * i + 8, :] for m in range(3)]
                for h in range(2):
                    v = q[8 * i:8 * i + 8, h * SLOTS:(h + 1) * SLOTS]
                    part[h][0] = part[h][0] + v
                    for m in range(3):
                        part[h][1 + m] = part[h][1 + m] + v * arm[m]
            for h in range(2):
                c = 2 * g + h
                pr = side_ref[n, 24 + c:25 + c, :]
                gap = [side_ref[n, 8 * m + c:8 * m + c + 1, :] for m in range(3)]
                push = [v * pr for v in part[h]]
                for m in range(3):
                    total = push[1 + m] + gap[m] * push[0]
                    reacts.append(total)
                    sums[m] = sums[m] + total
                    u, v = (m + 1) % 3, (m + 2) % 3
                    sums[3 + m] = sums[3 + m] + (push[1 + u] * gap[v] - push[1 + v] * gap[u])
        return reacts, sums

    def step(i, carry):
        picked = [order_ref[TOGETHER * i + n] for n in range(TOGETHER)]
        done = [one(t, n) for n, t in enumerate(picked)]
        for r in range(24):
            react_ref[r] = react_ref[r] + sum(d[0][r] for d in done)
        for t, d in zip(picked, done):
            for r in range(6):
                sums_ref[t, r:r + 1, :] = jnp.sum(d[1][r], axis=0, keepdims=True)
        return carry

    lax.fori_loop(0, (busy + TOGETHER - 1) // TOGETHER, step, 0)
    for r in range(24):
        force_ref[r % 3, r // 3:r // 3 + 1, :] = jnp.sum(react_ref[r], axis=0, keepdims=True)
    total = jnp.sum(sums_ref[...], axis=2)
    load_ref[...] = jnp.zeros_like(load_ref)
    for g in range(slots // CAPACITY):
        load_ref[g, 0:CAPACITY, 0:8] = total[CAPACITY * g:CAPACITY * g + CAPACITY, :]


def accel_kernel(own_ref, near_ref, coord_ref, left_ref, mid_ref, right_ref, force_ref, out_ref, press_ref, col_ref, line_ref):
    press_ref[0:16, :] = left_ref[16:32, :]
    press_ref[16:48, :] = mid_ref[...]
    press_ref[48:64, :] = right_ref[0:16, :]
    turned = mid_ref[...].T
    for a in range(2):
        for e in range(2):
            for f in range(2):
                r = (a * 4 + 1 + e) * 4 + 1 + f
                col_ref[4 * a + 2 * e + f] = jnp.broadcast_to(turned[:, r:r + 1], (SLOTS, SLOTS))
    steps = [(dx * 4 + dy) * 4 + dz for dx in (-1, 0, 1) for dy in (-1, 0, 1) for dz in (-1, 0, 1)]
    lane = lax.broadcasted_iota(jnp.int32, (32, SLOTS), 1)

    def cell(c, carry):
        a, e, f = c // 4, c // 2 % 2, c % 2
        w = ((a + 1) * 4 + e + 1) * 4 + f + 1

        def chunk(n):
            lhs = own_ref[c, n * 32:(n + 1) * 32, :]
            pi = col_ref[c, n * 32:(n + 1) * 32, :]
            acc = [jnp.zeros((32, SLOTS), F32) for _ in range(4)]
            for g in range(0, 27, 2):
                pair = steps[g:g + 2]
                rhs = [near_ref[w + s] for s in pair]
                rhs = jnp.concatenate(rhs, axis=1) if len(rhs) == 2 else rhs[0]
                q = jnp.maximum(jnp.dot(lhs, rhs, preferred_element_type=F32), 0.0)
                q = q * q
                for h, s in enumerate(pair):
                    weight = q[:, h * SLOTS:(h + 1) * SLOTS] * (pi + press_ref[pl.ds(w + s, 1), :])
                    acc[0] = acc[0] + weight
                    for m in range(3):
                        acc[1 + m] = acc[1 + m] + weight * coord_ref[w + s, m:m + 1, :]
            line = jnp.zeros((32, SLOTS), F32)
            for s in range(4):
                line = jnp.where(lane == s, jnp.sum(acc[s], axis=1, keepdims=True), line)
            line_ref[n * 32:(n + 1) * 32, :] = line

        for n in range(4):
            chunk(n)
        rows = line_ref[...].T
        live = coord_ref[w, 0:1, :] < 32.0
        for m in range(3):
            own = coord_ref[w, m:m + 1, :] * rows[0:1, :] - rows[1 + m:2 + m, :]
            own = jnp.where(live, own * (12.0 / SLOTS), 0.0)
            out_ref[m, a, e, pl.ds(f, 1), :] = own - force_ref[m, pl.ds(c, 1), :]
        return carry

    lax.fori_loop(0, 8, cell, 0, unroll=4)


def gather_kernel(slot_ref, got_ref, out_ref, pick_ref):
    bodies = out_ref.shape[1]
    pick_ref[...] = jnp.zeros_like(pick_ref)
    for b in range(bodies):
        place = slot_ref[b]
        pick_ref[b:b + 1, :] = got_ref[place // 8, pl.ds(place % 8, 1), :]
    out_ref[...] = pick_ref[...].T[0:6, 0:bodies] / BODY_PARTS


def vmem():
    return pl.BlockSpec(memory_space=pltpu.VMEM)


def smem():
    return pl.BlockSpec(memory_space=pltpu.SMEM)


def params():
    return pltpu.CompilerParams(vmem_limit_bytes=56 << 20)


def held(*values):
    return [pltpu.with_memory_space_constraint(v, pltpu.VMEM) for v in values]


def inner(*dims, dtype=F32):
    return pltpu.VMEM(dims, dtype)


def cost(giga):
    return pl.CostEstimate(flops=giga * 10**9 // 10, transcendentals=0, bytes_accessed=1 << 18)


def shift_ways(value, axis):
    count = lax.axis_size(axis)
    ups = [(i, i + 1) for i in range(count - 1)]
    downs = [(i + 1, i) for i in range(count - 1)]
    return lax.ppermute(value, axis, ups), lax.ppermute(value, axis, downs)


def swap_ways(value, axis):
    count = lax.axis_size(axis)
    inner_pairs = [(i, i ^ 1) for i in range(count)]
    outer_pairs = [(i, (i + 1 ^ 1) - 1) for i in range(1, count - 1)]
    return lax.ppermute(value, axis, inner_pairs), lax.ppermute(value, axis, outer_pairs)


def shaped(*dims, dtype=F32):
    return jax.ShapeDtypeStruct(dims, dtype)


def local(fluid_pos, fluid_count, body_shape, body_anchor, body_dest, body_cell):
    groups = lax.axis_size("gx")
    bodies = body_shape.shape[1]
    slots = groups * CAPACITY
    pos = pl.pallas_call(
        place_kernel,
        out_shape=inner(3, 8, SLOTS),
        in_specs=[vmem(), smem()],
        out_specs=vmem(),
        compiler_params=params(),
        name="place",
    )(fluid_pos, fluid_count)
    send, slot_of = pl.pallas_call(
        pack_kernel,
        out_shape=(inner(slots, 4, SLOTS), shaped(bodies, dtype=jnp.int32)),
        in_specs=[vmem(), vmem(), smem(), vmem()],
        out_specs=(vmem(), smem()),
        scratch_shapes=[pltpu.VMEM((SLOTS, SLOTS), F32), pltpu.SMEM((groups,), jnp.int32)],
        compiler_params=params(),
        cost_estimate=cost(4),
        name="pack",
    )(body_shape, jnp.swapaxes(body_anchor, 1, 2), body_dest.reshape(1, bodies), body_cell.T)
    low, high = swap_ways(pos, "body")
    low, high, send = lax.optimization_barrier((low, high, send))
    recv = lax.all_to_all(send.reshape(groups, CAPACITY, 4, SLOTS), "gx", 0, 0, tiled=True).reshape(slots, 4, SLOTS)
    line = jnp.stack([low, pos, high])
    low, high = swap_ways(line, "yz")
    sheet = jnp.stack([low, line, high]).reshape(9, 3, 8, SLOTS)
    left, right = shift_ways(sheet, "gx")
    near_mid, coord_mid, own_all, live, partial = pl.pallas_call(
        centre_kernel,
        out_shape=(
            inner(72, ROWS, SLOTS, dtype=BF16),
            inner(72, 8, SLOTS),
            inner(32, SLOTS, ROWS, dtype=BF16),
            inner(32, SLOTS),
            inner(SLOTS, SLOTS),
        ),
        in_specs=[vmem()],
        out_specs=(vmem(),) * 5,
        scratch_shapes=[
            pltpu.VMEM((ROWS * 8, SLOTS), F32),
            pltpu.VMEM((9, ROWS * 8, SLOTS), F32),
            pltpu.VMEM((64, SLOTS), F32),
        ],
        compiler_params=params(),
        cost_estimate=cost(60),
        name="centre",
    )(*held(sheet))
    rho, press, near, coord, own = pl.pallas_call(
        side_kernel,
        out_shape=(
            shaped(2, 2, 2, SLOTS),
            inner(32, SLOTS),
            inner(64, ROWS, SLOTS, dtype=BF16),
            inner(64, 8, SLOTS),
            inner(8, SLOTS, ROWS, dtype=BF16),
        ),
        in_specs=[vmem()] * 7,
        out_specs=(vmem(),) * 5,
        scratch_shapes=[
            pltpu.VMEM((72, ROWS, SLOTS), BF16),
            pltpu.VMEM((72, 8, SLOTS), F32),
            pltpu.VMEM((ROWS * 8, SLOTS), F32),
            pltpu.VMEM((64, SLOTS), F32),
            pltpu.VMEM((SLOTS, SLOTS), F32),
        ],
        compiler_params=params(),
        cost_estimate=cost(60),
        name="sides",
    )(*held(left, right, near_mid, coord_mid, own_all, live, partial))
    press_left, press_right = shift_ways(press, "gx")
    force, load = pl.pallas_call(
        body_kernel,
        out_shape=(inner(3, 8, SLOTS), inner(groups, 8, SLOTS)),
        in_specs=[vmem(), vmem(), vmem()],
        out_specs=(vmem(), vmem()),
        scratch_shapes=[
            pltpu.VMEM((8, SLOTS), F32),
            pltpu.VMEM((ROWS * slots, SLOTS), F32),
            pltpu.VMEM((8, SLOTS), F32),
            pltpu.VMEM((slots, 24, SLOTS), F32),
            pltpu.VMEM((TOGETHER, ROWS * 8, SLOTS), F32),
            pltpu.VMEM((TOGETHER, 32, SLOTS), F32),
            pltpu.VMEM((TOGETHER, 3, SLOTS, SLOTS), F32),
            pltpu.VMEM((24, 8, SLOTS), F32),
            pltpu.VMEM((slots, 8, SLOTS), F32),
            pltpu.SMEM((8, SLOTS), F32),
            pltpu.SMEM((slots + TOGETHER,), jnp.int32),
            pltpu.SemaphoreType.DMA,
        ],
        compiler_params=params(),
        cost_estimate=cost(60),
        name="bodies",
    )(*held(recv, pos, press))
    got = lax.all_to_all(load, "gx", 0, 0, tiled=True)
    accel = pl.pallas_call(
        accel_kernel,
        out_shape=shaped(3, 2, 2, 2, SLOTS),
        in_specs=[vmem()] * 7,
        out_specs=vmem(),
        scratch_shapes=[
            pltpu.VMEM((64, SLOTS), F32),
            pltpu.VMEM((8, SLOTS, SLOTS), F32),
            pltpu.VMEM((SLOTS, SLOTS), F32),
        ],
        compiler_params=params(),
        cost_estimate=cost(40),
        name="accel",
    )(*held(own, near, coord, press_left, press, press_right, force))
    body_load = pl.pallas_call(
        gather_kernel,
        out_shape=shaped(6, bodies),
        in_specs=[smem(), vmem()],
        out_specs=vmem(),
        scratch_shapes=[pltpu.VMEM((SLOTS, SLOTS), F32)],
        compiler_params=params(),
        cost_estimate=cost(1),
        name="collect",
    )(slot_of, *held(got))
    return rho, accel, body_load


def solution(mesh):
    in_specs = (
        P(None, "gx", "yz", "body", None),
        P("gx", "yz", "body"),
        P(None, ("gx", "yz", "body"), None),
        P(None, ("gx", "yz", "body"), None),
        P(("gx", "yz", "body"), None),
        P(("gx", "yz", "body"), None),
    )
    out_specs = (
        P("gx", "yz", "body", None),
        P(None, "gx", "yz", "body", None),
        P(None, ("gx", "yz", "body")),
    )
    return jax.shard_map(local, mesh=mesh, in_specs=in_specs, out_specs=out_specs, check_vma=False)
```

```python
import jax
import jax.numpy as jnp
from jax import lax
from jax.experimental import pallas as pl
from jax.experimental.pallas import tpu as pltpu
from jax.sharding import PartitionSpec as P

SLOTS = 128
BODY_PARTS = 128
CAPACITY = 3
FAR = 64.0
TOGETHER = 24
ROWS = 32
F32 = jnp.float32
BF16 = jnp.bfloat16


def split3(v):
    high = v.astype(BF16).astype(F32)
    rest = v - high
    mid = rest.astype(BF16).astype(F32)
    return high, mid, rest - mid


def near_rows(coords):
    rows = []
    norm = 0.0
    for v in coords:
        h, m, l = split3(v)
        rows += [h, m, h, l, h, m]
        norm = norm + v * v
    one = jnp.ones_like(norm)
    return rows + list(split3(-norm)) + [one, one, one]


def own_rows(coords):
    rows = []
    norm = 0.0
    for v in coords:
        h, m, l = split3(2.0 * v)
        rows += [h, h, m, h, l, m]
        norm = norm + v * v
    one = jnp.ones_like(norm)
    return rows + [one, one, one] + list(split3(1.0 - norm))


def place_kernel(pos_ref, count_ref, out_ref):
    lane = lax.broadcasted_iota(jnp.int32, (2, SLOTS), 1)
    row = lax.broadcasted_iota(jnp.int32, (2, SLOTS), 0)
    for a in range(2):
        for e in range(2):
            count = jnp.where(row == 0, count_ref[a, e, 0], count_ref[a, e, 1])
            live = lane < count
            base = 4 * a + 2 * e
            out_ref[0, base:base + 2, :] = jnp.where(live, pos_ref[0, a, e], FAR)
            out_ref[1, base:base + 2, :] = pos_ref[1, a, e]
            out_ref[2, base:base + 2, :] = pos_ref[2, a, e]


def pack_kernel(shape_ref, anchor_ref, dest_ref, cell_ref, send_ref, slot_ref, extra_ref, tally_ref):
    bodies = shape_ref.shape[1]
    groups = tally_ref.shape[0]
    send_ref[...] = jnp.zeros_like(send_ref)
    extra_ref[...] = jnp.zeros_like(extra_ref)
    first = cell_ref[0:1, :]
    for m in range(3):
        rows = [anchor_ref[m, k:k + 1, :] for k in range(8)]
        for bit in (1, 2, 4):
            flip = (first & bit) > 0
            rows = [jnp.where(flip, rows[k ^ bit], rows[k]) for k in range(8)]
        for k in range(8):
            extra_ref[8 * m + k:8 * m + k + 1, 0:bodies] = rows[k]
    extra_ref[24:32, :] = jnp.ones((8, SLOTS), F32)
    extra_ref[...] = extra_ref[...].T
    for g in range(groups):
        tally_ref[g] = 0
    for b in range(bodies):
        dest = dest_ref[0, b]
        rank = tally_ref[dest]
        tally_ref[dest] = rank + 1
        slot_ref[b] = dest * 8 + rank
        slot = dest * CAPACITY + rank
        send_ref[slot, 0:3, :] = shape_ref[:, b, :]
        send_ref[slot, 3:4, :] = extra_ref[b:b + 1, :]


def density_kernel(left_ref, mid_ref, right_ref, rho_ref, press_ref, near_out, coord_out, own_out, near_ref, coord_ref, own_ref, fb_ref, fa_ref, fr_ref, live_ref, col_ref):
    index = [lax.axis_index(n) for n in ("gx", "yz", "body")]
    size = [lax.axis_size(n) for n in ("gx", "yz", "body")]
    sub = lax.broadcasted_iota(jnp.int32, (8, SLOTS), 0)
    part = [sub // 4, sub // 2 % 2, sub % 2]
    fb_ref[...] = jnp.zeros_like(fb_ref)
    fa_ref[...] = jnp.zeros_like(fa_ref)
    fr_ref[...] = jnp.zeros_like(fr_ref)

    def block(t, carry):
        by = t // 3
        bz = t % 3
        ny = index[1] + by - 1
        nz = index[2] + bz - 1
        inside = (ny >= 0) & (ny < size[1]) & (nz >= 0) & (nz < size[2])
        off_y = (part[1] + 2 * by - 3).astype(F32)
        off_z = (part[2] + 2 * bz - 3).astype(F32)
        for kind in range(2):
            if kind == 0:
                raw = [mid_ref[t, m] for m in range(3)]
                wx = part[0] + 1
                ok = jnp.full((8, SLOTS), inside)
            else:
                raw = [jnp.where(sub >= 4, left_ref[t, m], right_ref[t, m]) for m in range(3)]
                wx = 3 - 3 * part[0]
                ok = jnp.where(sub >= 4, index[0], size[0] - 1 - index[0]) > 0
                ok = ok & inside
            coords = [
                jnp.where(ok, raw[0], FAR) + (wx - 2).astype(F32),
                raw[1] + off_y,
                raw[2] + off_z,
            ]
            for r, v in enumerate(near_rows(coords)):
                fb_ref[8 * r:8 * r + 8, :] = v
            for m in range(3):
                fr_ref[8 * m:8 * m + 8, :] = coords[m]
            if kind == 0:
                for r, v in enumerate(own_rows(coords)):
                    fa_ref[t, 8 * r:8 * r + 8, :] = v
            for c in range(8):
                a, e, f = c // 4, c // 2 % 2, c % 2
                at_x = 1 + a if kind == 0 else 3 - 3 * a
                w = (at_x * 6 + 2 * by + e) * 6 + 2 * bz + f
                near_ref[w] = fb_ref[pl.ds(c, ROWS, stride=8), :].astype(BF16)
                coord_ref[w] = fr_ref[pl.ds(c, 8, stride=8), :]
        return carry

    lax.fori_loop(0, 9, block, 0)

    def turn(r, carry):
        wy = r // 4 % 4 + 1
        wz = r % 4 + 1
        t = wy // 2 * 3 + wz // 2
        c = r // 16 * 4 + wy % 2 * 2 + wz % 2
        own_ref[r] = fa_ref[t, pl.ds(c, ROWS, stride=8), :].T.astype(BF16)
        w = ((r // 16 + 1) * 6 + wy) * 6 + wz
        live_ref[pl.ds(r, 1), :] = coord_ref[w, 0:1, :]
        return carry

    lax.fori_loop(0, 32, turn, 0, unroll=16)
    for i in range(16):
        w = ((i // 4) * 6 + i % 4 + 1) * 6 + 1
        near_out[4 * i:4 * i + 4] = near_ref[w:w + 4]
        coord_out[4 * i:4 * i + 4] = coord_ref[w:w + 4]
    for a in range(2):
        for e in range(2):
            r = (a * 4 + 1 + e) * 4 + 1
            own_out[4 * a + 2 * e:4 * a + 2 * e + 2] = own_ref[r:r + 2]
    col_ref[...] = jnp.zeros_like(col_ref)
    lane = lax.broadcasted_iota(jnp.int32, (SLOTS, SLOTS), 1)

    def cell(r, carry):
        w = ((r // 16 + 1) * 6 + r // 4 % 4 + 1) * 6 + r % 4 + 1
        lhs = own_ref[r]
        acc = jnp.zeros((SLOTS, SLOTS), F32)
        steps = [(dx * 6 + dy) * 6 + dz for dx in (-1, 0, 1) for dy in (-1, 0, 1) for dz in (-1, 0, 1)]
        for g in range(0, 27, 2):
            pair = steps[g:g + 2]
            rhs = [near_ref[w + s] for s in pair]
            rhs = jnp.concatenate(rhs, axis=1) if len(rhs) == 2 else rhs[0]
            q = jnp.maximum(jnp.dot(lhs, rhs, preferred_element_type=F32), 0.0)
            q = q * q * q
            for h in range(len(pair)):
                acc = acc + q[:, h * SLOTS:(h + 1) * SLOTS]
        total = jnp.sum(acc, axis=1, keepdims=True)
        col_ref[...] = jnp.where(lane == r, total, col_ref[...])
        return carry

    lax.fori_loop(0, 32, cell, 0, unroll=16)
    live = live_ref[...] < 32.0
    density = jnp.where(live, col_ref[...].T[0:32, :] / (SLOTS / 2.0), 0.0)
    safe = jnp.where(live, density, 1.0)
    press_ref[...] = jnp.where(live, (density - 1.0) / (safe * safe), 0.0)
    for a in range(2):
        for e in range(2):
            r = (a * 4 + 1 + e) * 4 + 1
            rho_ref[a, e] = density[r:r + 2, :]


def body_kernel(recv_ref, pos_ref, press_ref, force_ref, load_ref, list_ref, fa_ref, anchor_ref, near_ref, side_ref, half_ref, arm_ref, sums_ref):
    slots = recv_ref.shape[0]
    blank = jnp.zeros((8, SLOTS), F32)
    near_ref[:, 192:, :] = jnp.zeros((TOGETHER, 64, SLOTS), F32)
    force_ref[...] = jnp.zeros_like(force_ref)
    sums_ref[...] = jnp.zeros_like(sums_ref)
    fa_ref[24 * slots:, :] = jnp.zeros((8 * slots, SLOTS), F32)
    extras = jnp.concatenate([recv_ref[:, 3, :], jnp.zeros((SLOTS - slots, SLOTS), F32)], axis=0).T
    shapes = [recv_ref[:, m, :] for m in range(3)]
    for r, v in enumerate(own_rows(shapes)):
        fa_ref[r * slots:(r + 1) * slots, :] = v
    pieces = [split3(v) for v in shapes]
    arm_ref[7 * slots:, :] = jnp.zeros((9 * slots, SLOTS), F32)
    for r, v in enumerate([jnp.ones_like(shapes[0])] + [p[0] for p in pieces] + [p[1] + p[2] for p in pieces]):
        arm_ref[r * slots:(r + 1) * slots, :] = v
    for t in range(slots):
        for m in range(4):
            anchor_ref[t, 8 * m:8 * m + 8, :] = jnp.broadcast_to(extras[8 * m:8 * m + 8, t:t + 1], (8, SLOTS))
    press = jnp.concatenate([press_ref[(a * 4 + 1 + e) * 4 + 1:(a * 4 + 1 + e) * 4 + 3, :] for a in range(2) for e in range(2)], axis=0)
    list_ref[...] = press * (24.0 / SLOTS)
    coords = [pos_ref[m] for m in range(3)]

    def one(t, n):
        gaps = [coords[m] - anchor_ref[t, 8 * m:8 * m + 8, :] for m in range(3)]
        for r, v in enumerate(near_rows(gaps)):
            near_ref[n, 8 * r:8 * r + 8, :] = v
        for m in range(3):
            side_ref[n, 8 * m:8 * m + 8, :] = -gaps[m]
        side_ref[n, 24:32, :] = list_ref[...] * anchor_ref[t, 24:32, :]
        lhs = fa_ref[pl.ds(t, ROWS, stride=slots), :].T.astype(BF16)
        arms = arm_ref[pl.ds(t, 16, stride=slots), :].astype(BF16)
        for g in range(4):
            rhs = jnp.concatenate(
                [near_ref[n, pl.ds(c, ROWS, stride=8), :].astype(BF16) for c in (2 * g, 2 * g + 1)], axis=1
            )
            q = jnp.maximum(jnp.dot(lhs, rhs, preferred_element_type=F32), 0.0)
            q = q * q
            top = q.astype(BF16)
            low = (q - top.astype(F32)).astype(BF16)
            got = jnp.dot(arms, top, preferred_element_type=F32) + jnp.dot(arms, low, preferred_element_type=F32)
            for h in range(2):
                half_ref[n, 16 * g + 8 * h:16 * g + 8 * h + 8, :] = got[0:8, h * SLOTS:(h + 1) * SLOTS]
        rows = [half_ref[n, pl.ds(r, 8, stride=8), :] for r in range(7)]
        factor = side_ref[n, 24:32, :]
        push = [rows[0] * factor] + [(rows[1 + m] + rows[4 + m]) * factor for m in range(3)]
        gap = [side_ref[n, 8 * m:8 * m + 8, :] for m in range(3)]
        reacts = [push[1 + m] + gap[m] * push[0] for m in range(3)]
        turns = []
        for m in range(3):
            u, v = (m + 1) % 3, (m + 2) % 3
            turns.append(push[1 + u] * gap[v] - push[1 + v] * gap[u])
        return reacts, reacts + turns

    def step(i, carry):
        picked = [TOGETHER * i + n for n in range(TOGETHER)]
        done = [one(t, n) for n, t in enumerate(picked)]
        for m in range(3):
            force_ref[m] = force_ref[m] + sum(d[0][m] for d in done)
        for t, d in zip(picked, done):
            for r in range(6):
                sums_ref[t, r:r + 1, :] = jnp.sum(d[1][r], axis=0, keepdims=True)
        return carry

    lax.fori_loop(0, slots // TOGETHER, step, 0)
    total = jnp.sum(sums_ref[...], axis=2)
    load_ref[...] = jnp.zeros_like(load_ref)
    for g in range(slots // CAPACITY):
        load_ref[g, 0:CAPACITY, 0:8] = total[CAPACITY * g:CAPACITY * g + CAPACITY, :]


def accel_kernel(own_ref, near_ref, coord_ref, left_ref, mid_ref, right_ref, force_ref, out_ref, press_ref, col_ref, line_ref):
    press_ref[0:16, :] = left_ref[16:32, :]
    press_ref[16:48, :] = mid_ref[...]
    press_ref[48:64, :] = right_ref[0:16, :]
    turned = mid_ref[...].T
    for a in range(2):
        for e in range(2):
            for f in range(2):
                r = (a * 4 + 1 + e) * 4 + 1 + f
                col_ref[4 * a + 2 * e + f] = jnp.broadcast_to(turned[:, r:r + 1], (SLOTS, SLOTS))
    steps = [(dx * 4 + dy) * 4 + dz for dx in (-1, 0, 1) for dy in (-1, 0, 1) for dz in (-1, 0, 1)]
    lane = lax.broadcasted_iota(jnp.int32, (32, SLOTS), 1)

    def cell(c, carry):
        a, e, f = c // 4, c // 2 % 2, c % 2
        w = ((a + 1) * 4 + e + 1) * 4 + f + 1

        def chunk(n):
            lhs = own_ref[c, n * 32:(n + 1) * 32, :]
            pi = col_ref[c, n * 32:(n + 1) * 32, :]
            acc = [jnp.zeros((32, SLOTS), F32) for _ in range(4)]
            for g in range(0, 27, 2):
                pair = steps[g:g + 2]
                rhs = [near_ref[w + s] for s in pair]
                rhs = jnp.concatenate(rhs, axis=1) if len(rhs) == 2 else rhs[0]
                q = jnp.maximum(jnp.dot(lhs, rhs, preferred_element_type=F32), 0.0)
                q = q * q
                for h, s in enumerate(pair):
                    weight = q[:, h * SLOTS:(h + 1) * SLOTS] * (pi + press_ref[pl.ds(w + s, 1), :])
                    acc[0] = acc[0] + weight
                    for m in range(3):
                        acc[1 + m] = acc[1 + m] + weight * coord_ref[w + s, m:m + 1, :]
            line = jnp.zeros((32, SLOTS), F32)
            for s in range(4):
                line = jnp.where(lane == s, jnp.sum(acc[s], axis=1, keepdims=True), line)
            line_ref[n * 32:(n + 1) * 32, :] = line

        for n in range(4):
            chunk(n)
        rows = line_ref[...].T
        live = coord_ref[w, 0:1, :] < 32.0
        for m in range(3):
            own = coord_ref[w, m:m + 1, :] * rows[0:1, :] - rows[1 + m:2 + m, :]
            own = jnp.where(live, own * (12.0 / SLOTS), 0.0)
            out_ref[m, a, e, pl.ds(f, 1), :] = own - force_ref[m, pl.ds(c, 1), :]
        return carry

    lax.fori_loop(0, 8, cell, 0, unroll=8)


def gather_kernel(slot_ref, got_ref, out_ref, pick_ref):
    bodies = out_ref.shape[1]
    for b in range(bodies):
        place = slot_ref[b]
        pick_ref[b:b + 1, :] = got_ref[place // 8, pl.ds(place % 8, 1), :]
    out_ref[...] = pick_ref[...].T[0:6, :] / BODY_PARTS


def vmem():
    return pl.BlockSpec(memory_space=pltpu.VMEM)


def smem():
    return pl.BlockSpec(memory_space=pltpu.SMEM)


def params():
    return pltpu.CompilerParams(vmem_limit_bytes=56 << 20)


def held(*values):
    return [pltpu.with_memory_space_constraint(v, pltpu.VMEM) for v in values]


def inner(*dims, dtype=F32):
    return pltpu.VMEM(dims, dtype)


def cost(giga):
    return pl.CostEstimate(flops=giga * 10**9 // 10, transcendentals=0, bytes_accessed=1 << 18)


def both_ways(value, axis):
    count = lax.axis_size(axis)
    ups = [(i, i + 1) for i in range(count - 1)]
    downs = [(i + 1, i) for i in range(count - 1)]
    return lax.ppermute(value, axis, ups), lax.ppermute(value, axis, downs)


def shaped(*dims, dtype=F32):
    return jax.ShapeDtypeStruct(dims, dtype)


def local(fluid_pos, fluid_count, body_shape, body_anchor, body_dest, body_cell):
    groups = lax.axis_size("gx")
    bodies = body_shape.shape[1]
    slots = groups * CAPACITY
    pos = pl.pallas_call(
        place_kernel,
        out_shape=inner(3, 8, SLOTS),
        in_specs=[vmem(), smem()],
        out_specs=vmem(),
        compiler_params=params(),
        name="place",
    )(fluid_pos, fluid_count)
    send, slot_of = pl.pallas_call(
        pack_kernel,
        out_shape=(inner(slots, 4, SLOTS), shaped(bodies, dtype=jnp.int32)),
        in_specs=[vmem(), vmem(), smem(), vmem()],
        out_specs=(vmem(), smem()),
        scratch_shapes=[pltpu.VMEM((SLOTS, SLOTS), F32), pltpu.SMEM((groups,), jnp.int32)],
        compiler_params=params(),
        cost_estimate=cost(4),
        name="pack",
    )(body_shape, jnp.swapaxes(body_anchor, 1, 2), body_dest.reshape(1, bodies), body_cell.T)
    low, high = both_ways(pos, "body")
    low, high, send = lax.optimization_barrier((low, high, send))
    recv = lax.all_to_all(send.reshape(groups, CAPACITY, 4, SLOTS), "gx", 0, 0, tiled=True).reshape(slots, 4, SLOTS)
    line = jnp.stack([low, pos, high])
    low, high = both_ways(line, "yz")
    sheet = jnp.stack([low, line, high]).reshape(9, 3, 8, SLOTS)
    left, right = both_ways(sheet, "gx")
    rho, press, near, coord, own = pl.pallas_call(
        density_kernel,
        out_shape=(
            shaped(2, 2, 2, SLOTS),
            inner(32, SLOTS),
            inner(64, ROWS, SLOTS, dtype=BF16),
            inner(64, 8, SLOTS),
            inner(8, SLOTS, ROWS, dtype=BF16),
        ),
        in_specs=[vmem()] * 3,
        out_specs=(vmem(),) * 5,
        scratch_shapes=[
            pltpu.VMEM((144, ROWS, SLOTS), BF16),
            pltpu.VMEM((144, 8, SLOTS), F32),
            pltpu.VMEM((32, SLOTS, ROWS), BF16),
            pltpu.VMEM((ROWS * 8, SLOTS), F32),
            pltpu.VMEM((9, ROWS * 8, SLOTS), F32),
            pltpu.VMEM((64, SLOTS), F32),
            pltpu.VMEM((32, SLOTS), F32),
            pltpu.VMEM((SLOTS, SLOTS), F32),
        ],
        compiler_params=params(),
        cost_estimate=cost(60),
        name="density",
    )(*held(left, sheet, right))
    press_left, press_right = both_ways(press, "gx")
    force, load = pl.pallas_call(
        body_kernel,
        out_shape=(inner(3, 8, SLOTS), inner(groups, 8, SLOTS)),
        in_specs=[vmem(), vmem(), vmem()],
        out_specs=(vmem(), vmem()),
        scratch_shapes=[
            pltpu.VMEM((8, SLOTS), F32),
            pltpu.VMEM((ROWS * slots, SLOTS), F32),
            pltpu.VMEM((slots, 32, SLOTS), F32),
            pltpu.VMEM((TOGETHER, ROWS * 8, SLOTS), F32),
            pltpu.VMEM((TOGETHER, 32, SLOTS), F32),
            pltpu.VMEM((TOGETHER, 64, SLOTS), F32),
            pltpu.VMEM((16 * slots, SLOTS), F32),
            pltpu.VMEM((slots, 8, SLOTS), F32),
        ],
        compiler_params=params(),
        cost_estimate=cost(60),
        name="bodies",
    )(*held(recv, pos, press))
    got = lax.all_to_all(load, "gx", 0, 0, tiled=True)
    accel = pl.pallas_call(
        accel_kernel,
        out_shape=shaped(3, 2, 2, 2, SLOTS),
        in_specs=[vmem()] * 7,
        out_specs=vmem(),
        scratch_shapes=[
            pltpu.VMEM((64, SLOTS), F32),
            pltpu.VMEM((8, SLOTS, SLOTS), F32),
            pltpu.VMEM((SLOTS, SLOTS), F32),
        ],
        compiler_params=params(),
        cost_estimate=cost(40),
        name="accel",
    )(*held(own, near, coord, press_left, press, press_right, force))
    body_load = pl.pallas_call(
        gather_kernel,
        out_shape=shaped(6, bodies),
        in_specs=[smem(), vmem()],
        out_specs=vmem(),
        scratch_shapes=[pltpu.VMEM((bodies, SLOTS), F32)],
        compiler_params=params(),
        cost_estimate=cost(1),
        name="collect",
    )(slot_of, *held(got))
    return rho, accel, body_load


def solution(mesh):
    in_specs = (
        P(None, "gx", "yz", "body", None),
        P("gx", "yz", "body"),
        P(None, ("gx", "yz", "body"), None),
        P(None, ("gx", "yz", "body"), None),
        P(("gx", "yz", "body"), None),
        P(("gx", "yz", "body"), None),
    )
    out_specs = (
        P("gx", "yz", "body", None),
        P(None, "gx", "yz", "body", None),
        P(None, ("gx", "yz", "body")),
    )
    return jax.shard_map(local, mesh=mesh, in_specs=in_specs, out_specs=out_specs, check_vma=False)
```

```python
import jax
import jax.numpy as jnp
from jax import lax
from jax.experimental import pallas as pl
from jax.experimental.pallas import tpu as pltpu
from jax.sharding import PartitionSpec as P

SLOTS = 128
BODY_PARTS = 128
CAPACITY = 3
FAR = 64.0
TOGETHER = 24
ROWS = 32
F32 = jnp.float32
BF16 = jnp.bfloat16


def split3(v):
    high = v.astype(BF16).astype(F32)
    rest = v - high
    mid = rest.astype(BF16).astype(F32)
    return high, mid, rest - mid


def near_rows(coords):
    rows = []
    norm = 0.0
    for v in coords:
        h, m, l = split3(v)
        rows += [h, m, h, l, h, m]
        norm = norm + v * v
    one = jnp.ones_like(norm)
    return rows + list(split3(-norm)) + [one, one, one]


def own_rows(coords):
    rows = []
    norm = 0.0
    for v in coords:
        h, m, l = split3(2.0 * v)
        rows += [h, h, m, h, l, m]
        norm = norm + v * v
    one = jnp.ones_like(norm)
    return rows + [one, one, one] + list(split3(1.0 - norm))


def place_kernel(pos_ref, count_ref, out_ref):
    lane = lax.broadcasted_iota(jnp.int32, (2, SLOTS), 1)
    row = lax.broadcasted_iota(jnp.int32, (2, SLOTS), 0)
    for a in range(2):
        for e in range(2):
            count = jnp.where(row == 0, count_ref[a, e, 0], count_ref[a, e, 1])
            live = lane < count
            base = 4 * a + 2 * e
            out_ref[0, base:base + 2, :] = jnp.where(live, pos_ref[0, a, e], FAR)
            out_ref[1, base:base + 2, :] = pos_ref[1, a, e]
            out_ref[2, base:base + 2, :] = pos_ref[2, a, e]


def pack_kernel(shape_ref, anchor_ref, dest_ref, cell_ref, send_ref, slot_ref, extra_ref, tally_ref):
    bodies = shape_ref.shape[1]
    groups = tally_ref.shape[0]
    send_ref[...] = jnp.zeros_like(send_ref)
    extra_ref[...] = jnp.zeros_like(extra_ref)
    first = cell_ref[0:1, :]
    for m in range(3):
        rows = [anchor_ref[m, k:k + 1, :] for k in range(8)]
        for bit in (1, 2, 4):
            flip = (first & bit) > 0
            rows = [jnp.where(flip, rows[k ^ bit], rows[k]) for k in range(8)]
        for k in range(8):
            extra_ref[8 * m + k:8 * m + k + 1, 0:bodies] = rows[k]
    extra_ref[24:32, :] = jnp.ones((8, SLOTS), F32)
    extra_ref[...] = extra_ref[...].T
    for g in range(groups):
        tally_ref[g] = 0
    for b in range(bodies):
        dest = dest_ref[0, b]
        rank = tally_ref[dest]
        tally_ref[dest] = rank + 1
        slot_ref[b] = dest * 8 + rank
        slot = dest * CAPACITY + rank
        send_ref[slot, 0:3, :] = shape_ref[:, b, :]
        send_ref[slot, 3:4, :] = extra_ref[b:b + 1, :]


def block_of(t):
    by = jnp.where(lax.axis_index("yz") % 2 == 1, t // 3, 2 - t // 3)
    bz = jnp.where(lax.axis_index("body") % 2 == 1, t % 3, 2 - t % 3)
    return by, bz


def density_kernel(left_ref, mid_ref, right_ref, rho_ref, press_ref, near_out, coord_out, own_out, near_ref, coord_ref, own_ref, fb_ref, fa_ref, fr_ref, live_ref, col_ref):
    index = [lax.axis_index(n) for n in ("gx", "yz", "body")]
    size = [lax.axis_size(n) for n in ("gx", "yz", "body")]
    sub = lax.broadcasted_iota(jnp.int32, (8, SLOTS), 0)
    part = [sub // 4, sub // 2 % 2, sub % 2]
    fb_ref[...] = jnp.zeros_like(fb_ref)
    fa_ref[...] = jnp.zeros_like(fa_ref)
    fr_ref[...] = jnp.zeros_like(fr_ref)

    def block(t, carry):
        by, bz = block_of(t)
        ny = index[1] + by - 1
        nz = index[2] + bz - 1
        inside = (ny >= 0) & (ny < size[1]) & (nz >= 0) & (nz < size[2])
        off_y = (part[1] + 2 * by - 3).astype(F32)
        off_z = (part[2] + 2 * bz - 3).astype(F32)
        for kind in range(2):
            if kind == 0:
                raw = [mid_ref[t, m] for m in range(3)]
                wx = part[0] + 1
                ok = jnp.full((8, SLOTS), inside)
            else:
                raw = [jnp.where(sub >= 4, left_ref[t, m], right_ref[t, m]) for m in range(3)]
                wx = 3 - 3 * part[0]
                ok = jnp.where(sub >= 4, index[0], size[0] - 1 - index[0]) > 0
                ok = ok & inside
            coords = [
                jnp.where(ok, raw[0], FAR) + (wx - 2).astype(F32),
                raw[1] + off_y,
                raw[2] + off_z,
            ]
            for r, v in enumerate(near_rows(coords)):
                fb_ref[8 * r:8 * r + 8, :] = v
            for m in range(3):
                fr_ref[8 * m:8 * m + 8, :] = coords[m]
            if kind == 0:
                for r, v in enumerate(own_rows(coords)):
                    fa_ref[by * 3 + bz, 8 * r:8 * r + 8, :] = v
            for c in range(8):
                a, e, f = c // 4, c // 2 % 2, c % 2
                at_x = 1 + a if kind == 0 else 3 - 3 * a
                w = (at_x * 6 + 2 * by + e) * 6 + 2 * bz + f
                near_ref[w] = fb_ref[pl.ds(c, ROWS, stride=8), :].astype(BF16)
                coord_ref[w] = fr_ref[pl.ds(c, 8, stride=8), :]
        return carry

    lax.fori_loop(0, 9, block, 0)

    def turn(r, carry):
        wy = r // 4 % 4 + 1
        wz = r % 4 + 1
        t = wy // 2 * 3 + wz // 2
        c = r // 16 * 4 + wy % 2 * 2 + wz % 2
        own_ref[r] = fa_ref[t, pl.ds(c, ROWS, stride=8), :].T.astype(BF16)
        w = ((r // 16 + 1) * 6 + wy) * 6 + wz
        live_ref[pl.ds(r, 1), :] = coord_ref[w, 0:1, :]
        return carry

    lax.fori_loop(0, 32, turn, 0, unroll=16)
    for i in range(16):
        w = ((i // 4) * 6 + i % 4 + 1) * 6 + 1
        near_out[4 * i:4 * i + 4] = near_ref[w:w + 4]
        coord_out[4 * i:4 * i + 4] = coord_ref[w:w + 4]
    for a in range(2):
        for e in range(2):
            r = (a * 4 + 1 + e) * 4 + 1
            own_out[4 * a + 2 * e:4 * a + 2 * e + 2] = own_ref[r:r + 2]
    col_ref[...] = jnp.zeros_like(col_ref)
    lane = lax.broadcasted_iota(jnp.int32, (SLOTS, SLOTS), 1)

    def cell(r, carry):
        w = ((r // 16 + 1) * 6 + r // 4 % 4 + 1) * 6 + r % 4 + 1
        lhs = own_ref[r]
        acc = jnp.zeros((SLOTS, SLOTS), F32)
        steps = [(dx * 6 + dy) * 6 + dz for dx in (-1, 0, 1) for dy in (-1, 0, 1) for dz in (-1, 0, 1)]
        for g in range(0, 27, 2):
            pair = steps[g:g + 2]
            rhs = [near_ref[w + s] for s in pair]
            rhs = jnp.concatenate(rhs, axis=1) if len(rhs) == 2 else rhs[0]
            q = jnp.maximum(jnp.dot(lhs, rhs, preferred_element_type=F32), 0.0)
            q = q * q * q
            for h in range(len(pair)):
                acc = acc + q[:, h * SLOTS:(h + 1) * SLOTS]
        total = jnp.sum(acc, axis=1, keepdims=True)
        col_ref[...] = jnp.where(lane == r, total, col_ref[...])
        return carry

    lax.fori_loop(0, 32, cell, 0, unroll=16)
    live = live_ref[...] < 32.0
    density = jnp.where(live, col_ref[...].T[0:32, :] / (SLOTS / 2.0), 0.0)
    safe = jnp.where(live, density, 1.0)
    press_ref[...] = jnp.where(live, (density - 1.0) / (safe * safe), 0.0)
    for a in range(2):
        for e in range(2):
            r = (a * 4 + 1 + e) * 4 + 1
            rho_ref[a, e] = density[r:r + 2, :]


def body_kernel(recv_ref, pos_ref, press_ref, force_ref, load_ref, list_ref, fa_ref, anchor_ref, near_ref, side_ref, half_ref, arm_ref, sums_ref):
    slots = recv_ref.shape[0]
    blank = jnp.zeros((8, SLOTS), F32)
    near_ref[:, 192:, :] = jnp.zeros((TOGETHER, 64, SLOTS), F32)
    force_ref[...] = jnp.zeros_like(force_ref)
    sums_ref[...] = jnp.zeros_like(sums_ref)
    fa_ref[24 * slots:, :] = jnp.zeros((8 * slots, SLOTS), F32)
    extras = jnp.concatenate([recv_ref[:, 3, :], jnp.zeros((SLOTS - slots, SLOTS), F32)], axis=0).T
    shapes = [recv_ref[:, m, :] for m in range(3)]
    for r, v in enumerate(own_rows(shapes)):
        fa_ref[r * slots:(r + 1) * slots, :] = v
    pieces = [split3(v) for v in shapes]
    arm_ref[7 * slots:, :] = jnp.zeros((9 * slots, SLOTS), F32)
    for r, v in enumerate([jnp.ones_like(shapes[0])] + [p[0] for p in pieces] + [p[1] + p[2] for p in pieces]):
        arm_ref[r * slots:(r + 1) * slots, :] = v
    for t in range(slots):
        for m in range(4):
            anchor_ref[t, 8 * m:8 * m + 8, :] = jnp.broadcast_to(extras[8 * m:8 * m + 8, t:t + 1], (8, SLOTS))
    press = jnp.concatenate([press_ref[(a * 4 + 1 + e) * 4 + 1:(a * 4 + 1 + e) * 4 + 3, :] for a in range(2) for e in range(2)], axis=0)
    list_ref[...] = press * (24.0 / SLOTS)
    coords = [pos_ref[m] for m in range(3)]

    def one(t, n):
        gaps = [coords[m] - anchor_ref[t, 8 * m:8 * m + 8, :] for m in range(3)]
        for r, v in enumerate(near_rows(gaps)):
            near_ref[n, 8 * r:8 * r + 8, :] = v
        for m in range(3):
            side_ref[n, 8 * m:8 * m + 8, :] = -gaps[m]
        side_ref[n, 24:32, :] = list_ref[...] * anchor_ref[t, 24:32, :]
        lhs = fa_ref[pl.ds(t, ROWS, stride=slots), :].T.astype(BF16)
        arms = arm_ref[pl.ds(t, 16, stride=slots), :].astype(BF16)
        for g in range(4):
            rhs = jnp.concatenate(
                [near_ref[n, pl.ds(c, ROWS, stride=8), :].astype(BF16) for c in (2 * g, 2 * g + 1)], axis=1
            )
            q = jnp.maximum(jnp.dot(lhs, rhs, preferred_element_type=F32), 0.0)
            q = q * q
            top = q.astype(BF16)
            low = (q - top.astype(F32)).astype(BF16)
            got = jnp.dot(arms, top, preferred_element_type=F32) + jnp.dot(arms, low, preferred_element_type=F32)
            for h in range(2):
                half_ref[n, 16 * g + 8 * h:16 * g + 8 * h + 8, :] = got[0:8, h * SLOTS:(h + 1) * SLOTS]
        rows = [half_ref[n, pl.ds(r, 8, stride=8), :] for r in range(7)]
        factor = side_ref[n, 24:32, :]
        push = [rows[0] * factor] + [(rows[1 + m] + rows[4 + m]) * factor for m in range(3)]
        gap = [side_ref[n, 8 * m:8 * m + 8, :] for m in range(3)]
        reacts = [push[1 + m] + gap[m] * push[0] for m in range(3)]
        turns = []
        for m in range(3):
            u, v = (m + 1) % 3, (m + 2) % 3
            turns.append(push[1 + u] * gap[v] - push[1 + v] * gap[u])
        return reacts, reacts + turns

    def step(i, carry):
        picked = [TOGETHER * i + n for n in range(TOGETHER)]
        done = [one(t, n) for n, t in enumerate(picked)]
        for m in range(3):
            force_ref[m] = force_ref[m] + sum(d[0][m] for d in done)
        for t, d in zip(picked, done):
            for r in range(6):
                sums_ref[t, r:r + 1, :] = jnp.sum(d[1][r], axis=0, keepdims=True)
        return carry

    lax.fori_loop(0, slots // TOGETHER, step, 0)
    total = jnp.sum(sums_ref[...], axis=2)
    load_ref[...] = jnp.zeros_like(load_ref)
    for g in range(slots // CAPACITY):
        load_ref[g, 0:CAPACITY, 0:8] = total[CAPACITY * g:CAPACITY * g + CAPACITY, :]


def accel_kernel(own_ref, near_ref, coord_ref, left_ref, mid_ref, right_ref, force_ref, out_ref, press_ref, col_ref, line_ref):
    press_ref[0:16, :] = left_ref[16:32, :]
    press_ref[16:48, :] = mid_ref[...]
    press_ref[48:64, :] = right_ref[0:16, :]
    turned = mid_ref[...].T
    for a in range(2):
        for e in range(2):
            for f in range(2):
                r = (a * 4 + 1 + e) * 4 + 1 + f
                col_ref[4 * a + 2 * e + f] = jnp.broadcast_to(turned[:, r:r + 1], (SLOTS, SLOTS))
    steps = [(dx * 4 + dy) * 4 + dz for dx in (-1, 0, 1) for dy in (-1, 0, 1) for dz in (-1, 0, 1)]
    lane = lax.broadcasted_iota(jnp.int32, (32, SLOTS), 1)

    def cell(c, carry):
        a, e, f = c // 4, c // 2 % 2, c % 2
        w = ((a + 1) * 4 + e + 1) * 4 + f + 1

        def chunk(n):
            lhs = own_ref[c, n * 32:(n + 1) * 32, :]
            pi = col_ref[c, n * 32:(n + 1) * 32, :]
            acc = [jnp.zeros((32, SLOTS), F32) for _ in range(4)]
            for g in range(0, 27, 2):
                pair = steps[g:g + 2]
                rhs = [near_ref[w + s] for s in pair]
                rhs = jnp.concatenate(rhs, axis=1) if len(rhs) == 2 else rhs[0]
                q = jnp.maximum(jnp.dot(lhs, rhs, preferred_element_type=F32), 0.0)
                q = q * q
                for h, s in enumerate(pair):
                    weight = q[:, h * SLOTS:(h + 1) * SLOTS] * (pi + press_ref[pl.ds(w + s, 1), :])
                    acc[0] = acc[0] + weight
                    for m in range(3):
                        acc[1 + m] = acc[1 + m] + weight * coord_ref[w + s, m:m + 1, :]
            line = jnp.zeros((32, SLOTS), F32)
            for s in range(4):
                line = jnp.where(lane == s, jnp.sum(acc[s], axis=1, keepdims=True), line)
            line_ref[n * 32:(n + 1) * 32, :] = line

        for n in range(4):
            chunk(n)
        rows = line_ref[...].T
        live = coord_ref[w, 0:1, :] < 32.0
        for m in range(3):
            own = coord_ref[w, m:m + 1, :] * rows[0:1, :] - rows[1 + m:2 + m, :]
            own = jnp.where(live, own * (12.0 / SLOTS), 0.0)
            out_ref[m, a, e, pl.ds(f, 1), :] = own - force_ref[m, pl.ds(c, 1), :]
        return carry

    lax.fori_loop(0, 8, cell, 0, unroll=8)


def gather_kernel(slot_ref, got_ref, out_ref, pick_ref):
    bodies = out_ref.shape[1]
    for b in range(bodies):
        place = slot_ref[b]
        pick_ref[b:b + 1, :] = got_ref[place // 8, pl.ds(place % 8, 1), :]
    out_ref[...] = pick_ref[...].T[0:6, :] / BODY_PARTS


def vmem():
    return pl.BlockSpec(memory_space=pltpu.VMEM)


def smem():
    return pl.BlockSpec(memory_space=pltpu.SMEM)


def params():
    return pltpu.CompilerParams(vmem_limit_bytes=56 << 20)


def held(*values):
    return [pltpu.with_memory_space_constraint(v, pltpu.VMEM) for v in values]


def inner(*dims, dtype=F32):
    return pltpu.VMEM(dims, dtype)


def cost(giga):
    return pl.CostEstimate(flops=giga * 10**9 // 10, transcendentals=0, bytes_accessed=1 << 18)


def both_ways(value, axis):
    count = lax.axis_size(axis)
    ups = [(i, i + 1) for i in range(count - 1)]
    downs = [(i + 1, i) for i in range(count - 1)]
    return lax.ppermute(value, axis, ups), lax.ppermute(value, axis, downs)


def swap_ways(value, axis):
    count = lax.axis_size(axis)
    inner_pairs = [(i, i ^ 1) for i in range(count)]
    outer_pairs = [(i, (i + 1 ^ 1) - 1) for i in range(1, count - 1)]
    return lax.ppermute(value, axis, inner_pairs), lax.ppermute(value, axis, outer_pairs)


def shaped(*dims, dtype=F32):
    return jax.ShapeDtypeStruct(dims, dtype)


def local(fluid_pos, fluid_count, body_shape, body_anchor, body_dest, body_cell):
    groups = lax.axis_size("gx")
    bodies = body_shape.shape[1]
    slots = groups * CAPACITY
    pos = pl.pallas_call(
        place_kernel,
        out_shape=inner(3, 8, SLOTS),
        in_specs=[vmem(), smem()],
        out_specs=vmem(),
        compiler_params=params(),
        name="place",
    )(fluid_pos, fluid_count)
    send, slot_of = pl.pallas_call(
        pack_kernel,
        out_shape=(inner(slots, 4, SLOTS), shaped(bodies, dtype=jnp.int32)),
        in_specs=[vmem(), vmem(), smem(), vmem()],
        out_specs=(vmem(), smem()),
        scratch_shapes=[pltpu.VMEM((SLOTS, SLOTS), F32), pltpu.SMEM((groups,), jnp.int32)],
        compiler_params=params(),
        cost_estimate=cost(4),
        name="pack",
    )(body_shape, jnp.swapaxes(body_anchor, 1, 2), body_dest.reshape(1, bodies), body_cell.T)
    low, high = swap_ways(pos, "body")
    low, high, send = lax.optimization_barrier((low, high, send))
    recv = lax.all_to_all(send.reshape(groups, CAPACITY, 4, SLOTS), "gx", 0, 0, tiled=True).reshape(slots, 4, SLOTS)
    line = jnp.stack([low, pos, high])
    low, high = swap_ways(line, "yz")
    sheet = jnp.stack([low, line, high]).reshape(9, 3, 8, SLOTS)
    left, right = both_ways(sheet, "gx")
    rho, press, near, coord, own = pl.pallas_call(
        density_kernel,
        out_shape=(
            shaped(2, 2, 2, SLOTS),
            inner(32, SLOTS),
            inner(64, ROWS, SLOTS, dtype=BF16),
            inner(64, 8, SLOTS),
            inner(8, SLOTS, ROWS, dtype=BF16),
        ),
        in_specs=[vmem()] * 3,
        out_specs=(vmem(),) * 5,
        scratch_shapes=[
            pltpu.VMEM((144, ROWS, SLOTS), BF16),
            pltpu.VMEM((144, 8, SLOTS), F32),
            pltpu.VMEM((32, SLOTS, ROWS), BF16),
            pltpu.VMEM((ROWS * 8, SLOTS), F32),
            pltpu.VMEM((9, ROWS * 8, SLOTS), F32),
            pltpu.VMEM((64, SLOTS), F32),
            pltpu.VMEM((32, SLOTS), F32),
            pltpu.VMEM((SLOTS, SLOTS), F32),
        ],
        compiler_params=params(),
        cost_estimate=cost(60),
        name="density",
    )(*held(left, sheet, right))
    press_left, press_right = both_ways(press, "gx")
    force, load = pl.pallas_call(
        body_kernel,
        out_shape=(inner(3, 8, SLOTS), inner(groups, 8, SLOTS)),
        in_specs=[vmem(), vmem(), vmem()],
        out_specs=(vmem(), vmem()),
        scratch_shapes=[
            pltpu.VMEM((8, SLOTS), F32),
            pltpu.VMEM((ROWS * slots, SLOTS), F32),
            pltpu.VMEM((slots, 32, SLOTS), F32),
            pltpu.VMEM((TOGETHER, ROWS * 8, SLOTS), F32),
            pltpu.VMEM((TOGETHER, 32, SLOTS), F32),
            pltpu.VMEM((TOGETHER, 64, SLOTS), F32),
            pltpu.VMEM((16 * slots, SLOTS), F32),
            pltpu.VMEM((slots, 8, SLOTS), F32),
        ],
        compiler_params=params(),
        cost_estimate=cost(60),
        name="bodies",
    )(*held(recv, pos, press))
    got = lax.all_to_all(load, "gx", 0, 0, tiled=True)
    accel = pl.pallas_call(
        accel_kernel,
        out_shape=shaped(3, 2, 2, 2, SLOTS),
        in_specs=[vmem()] * 7,
        out_specs=vmem(),
        scratch_shapes=[
            pltpu.VMEM((64, SLOTS), F32),
            pltpu.VMEM((8, SLOTS, SLOTS), F32),
            pltpu.VMEM((SLOTS, SLOTS), F32),
        ],
        compiler_params=params(),
        cost_estimate=cost(40),
        name="accel",
    )(*held(own, near, coord, press_left, press, press_right, force))
    body_load = pl.pallas_call(
        gather_kernel,
        out_shape=shaped(6, bodies),
        in_specs=[smem(), vmem()],
        out_specs=vmem(),
        scratch_shapes=[pltpu.VMEM((bodies, SLOTS), F32)],
        compiler_params=params(),
        cost_estimate=cost(1),
        name="collect",
    )(slot_of, *held(got))
    return rho, accel, body_load


def solution(mesh):
    in_specs = (
        P(None, "gx", "yz", "body", None),
        P("gx", "yz", "body"),
        P(None, ("gx", "yz", "body"), None),
        P(None, ("gx", "yz", "body"), None),
        P(("gx", "yz", "body"), None),
        P(("gx", "yz", "body"), None),
    )
    out_specs = (
        P("gx", "yz", "body", None),
        P(None, "gx", "yz", "body", None),
        P(None, ("gx", "yz", "body")),
    )
    return jax.shard_map(local, mesh=mesh, in_specs=in_specs, out_specs=out_specs, check_vma=False)
```

```python
import jax
import jax.numpy as jnp
from jax import lax
from jax.experimental import pallas as pl
from jax.experimental.pallas import tpu as pltpu
from jax.sharding import PartitionSpec as P

SLOTS = 128
BODY_PARTS = 128
CAPACITY = 3
FAR = 64.0
TOGETHER = 24
ROWS = 32
F32 = jnp.float32
BF16 = jnp.bfloat16


def split3(v):
    high = v.astype(BF16).astype(F32)
    rest = v - high
    mid = rest.astype(BF16).astype(F32)
    return high, mid, rest - mid


def near_rows(coords):
    rows = []
    norm = 0.0
    for v in coords:
        h, m, l = split3(v)
        rows += [h, m, h, l, h, m]
        norm = norm + v * v
    one = jnp.ones_like(norm)
    return rows + list(split3(-norm)) + [one, one, one]


def own_rows(coords):
    rows = []
    norm = 0.0
    for v in coords:
        h, m, l = split3(2.0 * v)
        rows += [h, h, m, h, l, m]
        norm = norm + v * v
    one = jnp.ones_like(norm)
    return rows + [one, one, one] + list(split3(1.0 - norm))


def place_kernel(pos_ref, count_ref, out_ref):
    lane = lax.broadcasted_iota(jnp.int32, (2, SLOTS), 1)
    row = lax.broadcasted_iota(jnp.int32, (2, SLOTS), 0)
    for a in range(2):
        for e in range(2):
            count = jnp.where(row == 0, count_ref[a, e, 0], count_ref[a, e, 1])
            live = lane < count
            base = 4 * a + 2 * e
            out_ref[0, base:base + 2, :] = jnp.where(live, pos_ref[0, a, e], FAR)
            out_ref[1, base:base + 2, :] = pos_ref[1, a, e]
            out_ref[2, base:base + 2, :] = pos_ref[2, a, e]


def pack_kernel(shape_ref, anchor_ref, dest_ref, cell_ref, send_ref, slot_ref, extra_ref, tally_ref):
    bodies = shape_ref.shape[1]
    groups = tally_ref.shape[0]
    send_ref[...] = jnp.zeros_like(send_ref)
    extra_ref[...] = jnp.zeros_like(extra_ref)
    first = cell_ref[0:1, :]
    for m in range(3):
        rows = [anchor_ref[m, k:k + 1, :] for k in range(8)]
        for bit in (1, 2, 4):
            flip = (first & bit) > 0
            rows = [jnp.where(flip, rows[k ^ bit], rows[k]) for k in range(8)]
        for k in range(8):
            extra_ref[8 * m + k:8 * m + k + 1, 0:bodies] = rows[k]
    extra_ref[24:32, :] = jnp.ones((8, SLOTS), F32)
    extra_ref[...] = extra_ref[...].T
    for g in range(groups):
        tally_ref[g] = 0
    for b in range(bodies):
        dest = dest_ref[0, b]
        rank = tally_ref[dest]
        tally_ref[dest] = rank + 1
        slot_ref[b] = rank * groups + dest
        slot = dest * CAPACITY + rank
        send_ref[slot, 0:3, :] = shape_ref[:, b, :]
        send_ref[slot, 3:4, :] = extra_ref[b:b + 1, :]


def density_kernel(left_ref, mid_ref, right_ref, rho_ref, press_ref, near_out, coord_out, own_out, near_ref, coord_ref, own_ref, fb_ref, fa_ref, fr_ref, live_ref, col_ref):
    index = [lax.axis_index(n) for n in ("gx", "yz", "body")]
    size = [lax.axis_size(n) for n in ("gx", "yz", "body")]
    sub = lax.broadcasted_iota(jnp.int32, (8, SLOTS), 0)
    part = [sub // 4, sub // 2 % 2, sub % 2]
    fb_ref[...] = jnp.zeros_like(fb_ref)
    fa_ref[...] = jnp.zeros_like(fa_ref)
    fr_ref[...] = jnp.zeros_like(fr_ref)

    def block(t, carry):
        by = t // 3
        bz = t % 3
        ny = index[1] + by - 1
        nz = index[2] + bz - 1
        inside = (ny >= 0) & (ny < size[1]) & (nz >= 0) & (nz < size[2])
        off_y = (part[1] + 2 * by - 3).astype(F32)
        off_z = (part[2] + 2 * bz - 3).astype(F32)
        for kind in range(2):
            if kind == 0:
                raw = [mid_ref[t, m] for m in range(3)]
                wx = part[0] + 1
                ok = jnp.full((8, SLOTS), inside)
            else:
                raw = [jnp.where(sub >= 4, left_ref[t, m], right_ref[t, m]) for m in range(3)]
                wx = 3 - 3 * part[0]
                ok = jnp.where(sub >= 4, index[0], size[0] - 1 - index[0]) > 0
                ok = ok & inside
            coords = [
                jnp.where(ok, raw[0], FAR) + (wx - 2).astype(F32),
                raw[1] + off_y,
                raw[2] + off_z,
            ]
            for r, v in enumerate(near_rows(coords)):
                fb_ref[8 * r:8 * r + 8, :] = v
            for m in range(3):
                fr_ref[8 * m:8 * m + 8, :] = coords[m]
            if kind == 0:
                for r, v in enumerate(own_rows(coords)):
                    fa_ref[t, 8 * r:8 * r + 8, :] = v
            for c in range(8):
                a, e, f = c // 4, c // 2 % 2, c % 2
                at_x = 1 + a if kind == 0 else 3 - 3 * a
                w = (at_x * 6 + 2 * by + e) * 6 + 2 * bz + f
                near_ref[w] = fb_ref[pl.ds(c, ROWS, stride=8), :].astype(BF16)
                coord_ref[w] = fr_ref[pl.ds(c, 8, stride=8), :]
        return carry

    lax.fori_loop(0, 9, block, 0)

    def turn(r, carry):
        wy = r // 4 % 4 + 1
        wz = r % 4 + 1
        t = wy // 2 * 3 + wz // 2
        c = r // 16 * 4 + wy % 2 * 2 + wz % 2
        own_ref[r] = fa_ref[t, pl.ds(c, ROWS, stride=8), :].T.astype(BF16)
        w = ((r // 16 + 1) * 6 + wy) * 6 + wz
        live_ref[pl.ds(r, 1), :] = coord_ref[w, 0:1, :]
        return carry

    lax.fori_loop(0, 32, turn, 0, unroll=16)
    for i in range(16):
        w = ((i // 4) * 6 + i % 4 + 1) * 6 + 1
        near_out[4 * i:4 * i + 4] = near_ref[w:w + 4]
        coord_out[4 * i:4 * i + 4] = coord_ref[w:w + 4]
    for a in range(2):
        for e in range(2):
            r = (a * 4 + 1 + e) * 4 + 1
            own_out[4 * a + 2 * e:4 * a + 2 * e + 2] = own_ref[r:r + 2]
    col_ref[...] = jnp.zeros_like(col_ref)
    lane = lax.broadcasted_iota(jnp.int32, (SLOTS, SLOTS), 1)

    def cell(r, carry):
        w = ((r // 16 + 1) * 6 + r // 4 % 4 + 1) * 6 + r % 4 + 1
        lhs = own_ref[r]
        acc = jnp.zeros((SLOTS, SLOTS), F32)
        steps = [(dx * 6 + dy) * 6 + dz for dx in (-1, 0, 1) for dy in (-1, 0, 1) for dz in (-1, 0, 1)]
        for g in range(0, 27, 2):
            pair = steps[g:g + 2]
            rhs = [near_ref[w + s] for s in pair]
            rhs = jnp.concatenate(rhs, axis=1) if len(rhs) == 2 else rhs[0]
            q = jnp.maximum(jnp.dot(lhs, rhs, preferred_element_type=F32), 0.0)
            q = q * q * q
            for h in range(len(pair)):
                acc = acc + q[:, h * SLOTS:(h + 1) * SLOTS]
        total = jnp.sum(acc, axis=1, keepdims=True)
        col_ref[...] = jnp.where(lane == r, total, col_ref[...])
        return carry

    lax.fori_loop(0, 32, cell, 0, unroll=16)
    live = live_ref[...] < 32.0
    density = jnp.where(live, col_ref[...].T[0:32, :] / (SLOTS / 2.0), 0.0)
    safe = jnp.where(live, density, 1.0)
    press_ref[...] = jnp.where(live, (density - 1.0) / (safe * safe), 0.0)
    for a in range(2):
        for e in range(2):
            r = (a * 4 + 1 + e) * 4 + 1
            rho_ref[a, e] = density[r:r + 2, :]


def body_kernel(recv_ref, pos_ref, press_ref, force_ref, load_ref, list_ref, fa_ref, anchor_ref, near_ref, side_ref, half_ref, arm_ref, sums_ref, wide_ref):
    slots = recv_ref.shape[0]
    blank = jnp.zeros((8, SLOTS), F32)
    near_ref[:, 192:, :] = jnp.zeros((TOGETHER, 64, SLOTS), F32)
    force_ref[...] = jnp.zeros_like(force_ref)
    sums_ref[...] = jnp.zeros_like(sums_ref)
    fa_ref[24 * slots:, :] = jnp.zeros((8 * slots, SLOTS), F32)
    extras = jnp.concatenate([recv_ref[:, 3, :], jnp.zeros((SLOTS - slots, SLOTS), F32)], axis=0).T
    shapes = [recv_ref[:, m, :] for m in range(3)]
    for r, v in enumerate(own_rows(shapes)):
        fa_ref[r * slots:(r + 1) * slots, :] = v
    pieces = [split3(v) for v in shapes]
    arm_ref[7 * slots:, :] = jnp.zeros((9 * slots, SLOTS), F32)
    for r, v in enumerate([jnp.ones_like(shapes[0])] + [p[0] for p in pieces] + [p[1] + p[2] for p in pieces]):
        arm_ref[r * slots:(r + 1) * slots, :] = v
    for t in range(slots):
        for m in range(4):
            anchor_ref[t, 8 * m:8 * m + 8, :] = jnp.broadcast_to(extras[8 * m:8 * m + 8, t:t + 1], (8, SLOTS))
    press = jnp.concatenate([press_ref[(a * 4 + 1 + e) * 4 + 1:(a * 4 + 1 + e) * 4 + 3, :] for a in range(2) for e in range(2)], axis=0)
    list_ref[...] = press * (24.0 / SLOTS)
    coords = [pos_ref[m] for m in range(3)]

    def one(t, n):
        gaps = [coords[m] - anchor_ref[t, 8 * m:8 * m + 8, :] for m in range(3)]
        for r, v in enumerate(near_rows(gaps)):
            near_ref[n, 8 * r:8 * r + 8, :] = v
        for m in range(3):
            side_ref[n, 8 * m:8 * m + 8, :] = -gaps[m]
        side_ref[n, 24:32, :] = list_ref[...] * anchor_ref[t, 24:32, :]
        lhs = fa_ref[pl.ds(t, ROWS, stride=slots), :].T.astype(BF16)
        arms = arm_ref[pl.ds(t, 16, stride=slots), :].astype(BF16)
        for g in range(4):
            rhs = jnp.concatenate(
                [near_ref[n, pl.ds(c, ROWS, stride=8), :].astype(BF16) for c in (2 * g, 2 * g + 1)], axis=1
            )
            q = jnp.maximum(jnp.dot(lhs, rhs, preferred_element_type=F32), 0.0)
            q = q * q
            top = q.astype(BF16)
            low = (q - top.astype(F32)).astype(BF16)
            got = jnp.dot(arms, top, preferred_element_type=F32) + jnp.dot(arms, low, preferred_element_type=F32)
            for h in range(2):
                half_ref[n, 16 * g + 8 * h:16 * g + 8 * h + 8, :] = got[0:8, h * SLOTS:(h + 1) * SLOTS]
        rows = [half_ref[n, pl.ds(r, 8, stride=8), :] for r in range(7)]
        factor = side_ref[n, 24:32, :]
        push = [rows[0] * factor] + [(rows[1 + m] + rows[4 + m]) * factor for m in range(3)]
        gap = [side_ref[n, 8 * m:8 * m + 8, :] for m in range(3)]
        reacts = [push[1 + m] + gap[m] * push[0] for m in range(3)]
        turns = []
        for m in range(3):
            u, v = (m + 1) % 3, (m + 2) % 3
            turns.append(push[1 + u] * gap[v] - push[1 + v] * gap[u])
        return reacts, reacts + turns

    def step(i, carry):
        picked = [TOGETHER * i + n for n in range(TOGETHER)]
        done = [one(t, n) for n, t in enumerate(picked)]
        for m in range(3):
            force_ref[m] = force_ref[m] + sum(d[0][m] for d in done)
        for t, d in zip(picked, done):
            for r in range(6):
                sums_ref[t, r:r + 1, :] = jnp.sum(d[1][r], axis=0, keepdims=True)
        return carry

    lax.fori_loop(0, slots // TOGETHER, step, 0)
    total = jnp.sum(sums_ref[...], axis=2)
    groups = slots // CAPACITY
    wide_ref[...] = jnp.concatenate([total, jnp.zeros((slots, SLOTS - 8), F32)], axis=1)
    mixed = sum(
        pltpu.roll(wide_ref[pl.ds(r, groups, stride=CAPACITY), :], 8 * r, 1) if r else wide_ref[pl.ds(0, groups, stride=CAPACITY), :]
        for r in range(CAPACITY)
    )
    for g in range(groups):
        load_ref[g] = mixed[g:g + 1, :]


def accel_kernel(own_ref, near_ref, coord_ref, left_ref, mid_ref, right_ref, force_ref, out_ref, press_ref, col_ref, line_ref):
    press_ref[0:16, :] = left_ref[16:32, :]
    press_ref[16:48, :] = mid_ref[...]
    press_ref[48:64, :] = right_ref[0:16, :]
    turned = mid_ref[...].T
    for a in range(2):
        for e in range(2):
            for f in range(2):
                r = (a * 4 + 1 + e) * 4 + 1 + f
                col_ref[4 * a + 2 * e + f] = jnp.broadcast_to(turned[:, r:r + 1], (SLOTS, SLOTS))
    steps = [(dx * 4 + dy) * 4 + dz for dx in (-1, 0, 1) for dy in (-1, 0, 1) for dz in (-1, 0, 1)]
    lane = lax.broadcasted_iota(jnp.int32, (32, SLOTS), 1)

    def cell(c, carry):
        a, e, f = c // 4, c // 2 % 2, c % 2
        w = ((a + 1) * 4 + e + 1) * 4 + f + 1

        def chunk(n):
            lhs = own_ref[c, n * 32:(n + 1) * 32, :]
            pi = col_ref[c, n * 32:(n + 1) * 32, :]
            acc = [jnp.zeros((32, SLOTS), F32) for _ in range(4)]
            for g in range(0, 27, 2):
                pair = steps[g:g + 2]
                rhs = [near_ref[w + s] for s in pair]
                rhs = jnp.concatenate(rhs, axis=1) if len(rhs) == 2 else rhs[0]
                q = jnp.maximum(jnp.dot(lhs, rhs, preferred_element_type=F32), 0.0)
                q = q * q
                for h, s in enumerate(pair):
                    weight = q[:, h * SLOTS:(h + 1) * SLOTS] * (pi + press_ref[pl.ds(w + s, 1), :])
                    acc[0] = acc[0] + weight
                    for m in range(3):
                        acc[1 + m] = acc[1 + m] + weight * coord_ref[w + s, m:m + 1, :]
            line = jnp.zeros((32, SLOTS), F32)
            for s in range(4):
                line = jnp.where(lane == s, jnp.sum(acc[s], axis=1, keepdims=True), line)
            line_ref[n * 32:(n + 1) * 32, :] = line

        for n in range(4):
            chunk(n)
        rows = line_ref[...].T
        live = coord_ref[w, 0:1, :] < 32.0
        for m in range(3):
            own = coord_ref[w, m:m + 1, :] * rows[0:1, :] - rows[1 + m:2 + m, :]
            own = jnp.where(live, own * (12.0 / SLOTS), 0.0)
            out_ref[m, a, e, pl.ds(f, 1), :] = own - force_ref[m, pl.ds(c, 1), :]
        return carry

    lax.fori_loop(0, 8, cell, 0, unroll=8)


def gather_kernel(slot_ref, got_ref, out_ref, pick_ref, roll_ref):
    bodies = out_ref.shape[1]
    groups = got_ref.shape[0]
    for g in range(groups):
        roll_ref[g:g + 1, :] = got_ref[g]
    for r in range(1, CAPACITY):
        roll_ref[r * groups:(r + 1) * groups, :] = pltpu.roll(roll_ref[0:groups, :], SLOTS - 8 * r, 1)
    for b in range(bodies):
        pick_ref[b:b + 1, :] = roll_ref[pl.ds(slot_ref[b], 1), :]
    out_ref[...] = pick_ref[...].T[0:6, :] / BODY_PARTS


def vmem():
    return pl.BlockSpec(memory_space=pltpu.VMEM)


def smem():
    return pl.BlockSpec(memory_space=pltpu.SMEM)


def params():
    return pltpu.CompilerParams(vmem_limit_bytes=56 << 20)


def held(*values):
    return [pltpu.with_memory_space_constraint(v, pltpu.VMEM) for v in values]


def inner(*dims, dtype=F32):
    return pltpu.VMEM(dims, dtype)


def cost(giga):
    return pl.CostEstimate(flops=giga * 10**9 // 10, transcendentals=0, bytes_accessed=1 << 18)


def both_ways(value, axis):
    count = lax.axis_size(axis)
    ups = [(i, i + 1) for i in range(count - 1)]
    downs = [(i + 1, i) for i in range(count - 1)]
    return lax.ppermute(value, axis, ups), lax.ppermute(value, axis, downs)


def shaped(*dims, dtype=F32):
    return jax.ShapeDtypeStruct(dims, dtype)


def local(fluid_pos, fluid_count, body_shape, body_anchor, body_dest, body_cell):
    groups = lax.axis_size("gx")
    bodies = body_shape.shape[1]
    slots = groups * CAPACITY
    pos = pl.pallas_call(
        place_kernel,
        out_shape=inner(3, 8, SLOTS),
        in_specs=[vmem(), smem()],
        out_specs=vmem(),
        compiler_params=params(),
        name="place",
    )(fluid_pos, fluid_count)
    send, slot_of = pl.pallas_call(
        pack_kernel,
        out_shape=(inner(slots, 4, SLOTS), shaped(bodies, dtype=jnp.int32)),
        in_specs=[vmem(), vmem(), smem(), vmem()],
        out_specs=(vmem(), smem()),
        scratch_shapes=[pltpu.VMEM((SLOTS, SLOTS), F32), pltpu.SMEM((groups,), jnp.int32)],
        compiler_params=params(),
        cost_estimate=cost(4),
        name="pack",
    )(body_shape, jnp.swapaxes(body_anchor, 1, 2), body_dest.reshape(1, bodies), body_cell.T)
    low, high = both_ways(pos, "body")
    low, high, send = lax.optimization_barrier((low, high, send))
    recv = lax.all_to_all(send.reshape(groups, CAPACITY, 4, SLOTS), "gx", 0, 0, tiled=True).reshape(slots, 4, SLOTS)
    line = jnp.stack([low, pos, high])
    low, high = both_ways(line, "yz")
    sheet = jnp.stack([low, line, high]).reshape(9, 3, 8, SLOTS)
    left, right = both_ways(sheet, "gx")
    rho, press, near, coord, own = pl.pallas_call(
        density_kernel,
        out_shape=(
            shaped(2, 2, 2, SLOTS),
            inner(32, SLOTS),
            inner(64, ROWS, SLOTS, dtype=BF16),
            inner(64, 8, SLOTS),
            inner(8, SLOTS, ROWS, dtype=BF16),
        ),
        in_specs=[vmem()] * 3,
        out_specs=(vmem(),) * 5,
        scratch_shapes=[
            pltpu.VMEM((144, ROWS, SLOTS), BF16),
            pltpu.VMEM((144, 8, SLOTS), F32),
            pltpu.VMEM((32, SLOTS, ROWS), BF16),
            pltpu.VMEM((ROWS * 8, SLOTS), F32),
            pltpu.VMEM((9, ROWS * 8, SLOTS), F32),
            pltpu.VMEM((64, SLOTS), F32),
            pltpu.VMEM((32, SLOTS), F32),
            pltpu.VMEM((SLOTS, SLOTS), F32),
        ],
        compiler_params=params(),
        cost_estimate=cost(60),
        name="density",
    )(*held(left, sheet, right))
    press_left, press_right = both_ways(press, "gx")
    force, load = pl.pallas_call(
        body_kernel,
        out_shape=(inner(3, 8, SLOTS), inner(groups, 1, SLOTS)),
        in_specs=[vmem(), vmem(), vmem()],
        out_specs=(vmem(), vmem()),
        scratch_shapes=[
            pltpu.VMEM((8, SLOTS), F32),
            pltpu.VMEM((ROWS * slots, SLOTS), F32),
            pltpu.VMEM((slots, 32, SLOTS), F32),
            pltpu.VMEM((TOGETHER, ROWS * 8, SLOTS), F32),
            pltpu.VMEM((TOGETHER, 32, SLOTS), F32),
            pltpu.VMEM((TOGETHER, 64, SLOTS), F32),
            pltpu.VMEM((16 * slots, SLOTS), F32),
            pltpu.VMEM((slots, 8, SLOTS), F32),
            pltpu.VMEM((slots, SLOTS), F32),
        ],
        compiler_params=params(),
        cost_estimate=cost(60),
        name="bodies",
    )(*held(recv, pos, press))
    got = lax.all_to_all(load, "gx", 0, 0, tiled=True)
    accel = pl.pallas_call(
        accel_kernel,
        out_shape=shaped(3, 2, 2, 2, SLOTS),
        in_specs=[vmem()] * 7,
        out_specs=vmem(),
        scratch_shapes=[
            pltpu.VMEM((64, SLOTS), F32),
            pltpu.VMEM((8, SLOTS, SLOTS), F32),
            pltpu.VMEM((SLOTS, SLOTS), F32),
        ],
        compiler_params=params(),
        cost_estimate=cost(40),
        name="accel",
    )(*held(own, near, coord, press_left, press, press_right, force))
    body_load = pl.pallas_call(
        gather_kernel,
        out_shape=shaped(6, bodies),
        in_specs=[smem(), vmem()],
        out_specs=vmem(),
        scratch_shapes=[pltpu.VMEM((bodies, SLOTS), F32), pltpu.VMEM((slots, SLOTS), F32)],
        compiler_params=params(),
        cost_estimate=cost(1),
        name="collect",
    )(slot_of, *held(got))
    return rho, accel, body_load


def solution(mesh):
    in_specs = (
        P(None, "gx", "yz", "body", None),
        P("gx", "yz", "body"),
        P(None, ("gx", "yz", "body"), None),
        P(None, ("gx", "yz", "body"), None),
        P(("gx", "yz", "body"), None),
        P(("gx", "yz", "body"), None),
    )
    out_specs = (
        P("gx", "yz", "body", None),
        P(None, "gx", "yz", "body", None),
        P(None, ("gx", "yz", "body")),
    )
    return jax.shard_map(local, mesh=mesh, in_specs=in_specs, out_specs=out_specs, check_vma=False)
```
